32 devices in a mesh: dp: 4 (over y, core), cells: 8 (over z, x).
Axes of the slice: x: 2, y: 2, z: 4, core: 2. Of those that a mesh axis runs over, the one named last changes fastest.
Arguments:
- jac_blocks: bfloat16 [32, 128, 8192], P('dp', None, 'cells'), may hold values from -6 to 6
- slot_cell_blocks: int32 [32, 64], P('dp', 'cells'), may hold values from 0 to 15, as said below
- live_counts: int32 [32, 8], P('dp', 'cells'), may hold values from 1 to 8, as said below
- eigen_basis: bfloat16 [16384, 1536], P('cells', 'dp'), may hold values from -0.0625 to 0.0625
- weights: float32 [4096], P(('dp', 'cells')), may hold values from 0.25 to 4
- residual: float32 [4096], P(('dp', 'cells')), may hold values from -6 to 6
Outputs:
- jq: float32 [4096, 1536], P(('dp', 'cells'))
- system: float32 [1536, 1536], P('cells')
- rhs: float32 [1536], P('cells')
The draws below stay inside these ranges and needn't reach their ends.
Inputs may be any that keep to these rules, and one draw needn't show every extreme that they name: `slot_cell_blocks`: within one data block and one slab, the 8 entries name distinct cell blocks; only the first live_counts entries are used. `live_counts`: every data block has 8 live slots in some slab.
All inputs are finite; a program needn't handle non-finite values.
Results may differ from the reference program's by a relative error of at most 0.0003.
Values may be sent and summed in bfloat16 or wider, within the bound.
A program may use at most 128 MiB of HBM per device.

```python
import math
import jax
import jax.numpy as jnp
from jax import lax

K = 1536
BLOCK = 128
SLOTS = 8
CB_DEV = 16
SLABS = 8
CELLS = 16384
NDATA = 4096
DBLOCKS = 32


def draw_slot_cell_blocks(key, part):
    keys = jax.random.split(key, DBLOCKS * SLABS)
    picks = jax.vmap(lambda k: jax.random.permutation(k, CB_DEV)[:SLOTS])(keys)
    return picks.reshape(DBLOCKS, SLABS * SLOTS).astype(jnp.int32)


def draw_live_counts(key, part):
    key_start = jax.random.fold_in(key, 11)
    key_center = jax.random.fold_in(key, 12)
    key_jitter = jax.random.fold_in(key, 13)
    region = jax.random.randint(key_start, (), 0, SLABS)
    spread = max(SLABS // 4, 1)
    centers = (region + jax.random.randint(key_center, (DBLOCKS, 1), 0, spread)) % SLABS
    slab_ids = jnp.arange(SLABS, dtype=jnp.int32)[None, :]
    gap = jnp.abs(slab_ids - centers)
    dist = jnp.minimum(gap, SLABS - gap)
    jitter = jax.random.randint(key_jitter, (DBLOCKS, SLABS), -1, 2)
    counts = SLOTS - dist * SLOTS // (SLABS // 2 + 1) + jitter
    counts = jnp.clip(counts, 1, SLOTS)
    counts = jnp.where(dist == 0, SLOTS, counts)
    return counts.astype(jnp.int32)


def block_levels(own_key, extent, cuts, low, top_value):
    def one(dim, shards_of):
        steps = jax.random.uniform(jax.random.fold_in(jax.random.fold_in(own_key, 6), dim), (shards_of,), jnp.float32, low / len(cuts), top_value / len(cuts))
        return jnp.repeat(jnp.exp(steps), extent[dim] // shards_of).reshape((-1,) + (1,) * (len(extent) - dim - 1))

    gain = one(*cuts[0])
    for cut in cuts[1:]:
        gain = gain * one(*cut)
    return gain


def gaussian(key, extent, scale, limit, pieces=(), held_as=jnp.bfloat16):
    array = scale * jax.random.normal(key, extent, jnp.float32)
    if pieces:
        array = array * block_levels(key, extent, pieces, -0.22, 0.18)
    return jnp.clip(array, -limit, limit).astype(held_as)


def setup_inputs(seed: int = 0) -> dict:
    key_list = jax.random.split(jax.random.key(seed), 7)
    jac_blocks = gaussian(key_list[0], (DBLOCKS, BLOCK, SLABS * SLOTS * BLOCK), 1.0, 6.0, ((0, 4), (2, 8)))
    slot_cell_blocks = draw_slot_cell_blocks(jax.random.fold_in(key_list[6], 71), 0)
    live_counts = draw_live_counts(jax.random.fold_in(key_list[6], 71), 0)
    eigen_basis = gaussian(key_list[3], (CELLS, K), (BLOCK * SLOTS * SLABS) ** -0.5, 0.0625, ((0, 8), (1, 4)))
    weights = jnp.clip(jnp.exp(math.log(4.0) - 2.7725887 * jax.random.uniform(key_list[4], (NDATA,), jnp.float32) ** block_levels(key_list[4], (NDATA,), ((0, 32),), -0.2, 0.2)), 0.25, 4.0)
    residual = gaussian(key_list[5], (NDATA,), 1.0, 6.0, ((0, 32),), jnp.float32)
    return {"jac_blocks": jac_blocks, "slot_cell_blocks": slot_cell_blocks, "live_counts": live_counts, "eigen_basis": eigen_basis, "weights": weights, "residual": residual}


def reference(jac_blocks, slot_cell_blocks, live_counts, eigen_basis, weights, residual):
    block_width = eigen_basis.shape[1]
    stacked_blocks = eigen_basis.reshape(CELLS // BLOCK, BLOCK, block_width)
    slot_ids = jnp.arange(SLABS * SLOTS, dtype=jnp.int32)
    slab_base = slot_ids // SLOTS * CB_DEV
    slot_pos = slot_ids % SLOTS

    def one_block(items):
        jacobian_row, column_range, active_slot = items
        retain_flag = (slot_pos < jnp.repeat(active_slot, SLOTS)).astype(jnp.bfloat16)
        masked_entries = (jacobian_row.reshape(BLOCK, SLABS * SLOTS, BLOCK) * retain_flag[None, :, None]).reshape(BLOCK, SLABS * SLOTS * BLOCK)
        selected_rows = stacked_blocks[(column_range + slab_base).astype(jnp.int32)].reshape(SLABS * SLOTS * BLOCK, block_width)
        return jnp.dot(masked_entries, selected_rows, preferred_element_type=jnp.float32)
    jq = lax.map(one_block, (jac_blocks, slot_cell_blocks, live_counts)).reshape(NDATA, block_width)
    weighted = jq * weights[:, None]
    gram = lax.dot_general(jq, weighted, (((0,), (0,)), ((), ())), precision=lax.Precision.HIGHEST) / NDATA
    system = gram + jnp.eye(block_width, dtype=jnp.float32)
    rhs = lax.dot_general(jq, weights * residual, (((0,), (0,)), ((), ())), precision=lax.Precision.HIGHEST) / math.sqrt(NDATA)
    return (jq, system, rhs)
```

```python
import functools
import math

import jax
import jax.numpy as jnp
from jax import lax
from jax.experimental import pallas as pl
from jax.experimental.pallas import tpu as pltpu
from jax.sharding import PartitionSpec as P

LANES = 128
SOURCE = {1: 0, 2: 0, 4: 0, 6: 4, 3: 2, 5: 4, 7: 6}


def code(value):
    top = jnp.maximum(jnp.max(jnp.abs(value), axis=0, keepdims=True), 1e-30)
    whole = jnp.round(value * (32767.0 / top))
    return whole.astype(jnp.int32).astype(jnp.int16), top * (1.0 / 32767.0)


def decode(whole, unit):
    return whole.astype(jnp.int32).astype(jnp.float32) * unit


def fused(
    n_cells, ndata, units, order, chunks, aligned,
    slots, live, jac_in, basis_in, weights, residual,
    jq, system, rhs,
    own_basis, peer_basis, gy, jac, sel, xq, xs, xrq, xrs, zrq, zrs, acc, uq, us, u, v,
    tq, tcol, prod, gbufs, sysb, vr, sq, su,
    in_s, b_s, b_r, y_s, y_r, w_s, w_r, x_s, x_r, z_s, z_r, u_s, u_r, t_s, t_r,
    vz_s, vz_r, s_s, s_r, g_sems,
):
    f32 = jnp.float32
    half = n_cells // 2
    tile = jac.shape[1]
    slot_count = jac.shape[2] // tile
    width = basis_in.shape[2]
    full = uq.shape[2]
    own_rows = sysb.shape[0]
    k_half = own_basis.shape[0] // 2
    window = vr.shape[2]
    me, cell = lax.axis_index("dp"), lax.axis_index("cells")
    core, y = me % 2, me // 2
    core_peer = y * 2 + 1 - core
    y_peer = (1 - y) * 2 + core
    far_peer = (1 - y) * 2 + 1 - core
    sources = (me, core_peer, y_peer, far_peer)
    x, line = cell % 2, cell // 2
    x_cell = line * 2 + 1 - x

    def remote(src, dst, send, recv, dp, to_cell):
        return pltpu.make_async_remote_copy(
            src_ref=src, dst_ref=dst, send_sem=send, recv_sem=recv,
            device_id=(dp, to_cell), device_id_type=pl.DeviceIdType.MESH,
        )

    def pair(src, dst, send, recv, at, to, dp, to_cell):
        return [
            remote(src[i], dst[i], send.at[(i, *at)], recv.at[(i, *to)], dp, to_cell)
            for i in range(2)
        ]

    def each(verb, copies):
        for copy in copies:
            getattr(copy, verb)()

    def when(condition, run):
        if condition is None:
            run()
        else:
            pl.when(condition)(run)

    load_basis = pltpu.make_async_copy(basis_in, own_basis, in_s.at[0])
    load_jac = pltpu.make_async_copy(jac_in, jac, in_s.at[1])
    load_basis.start()
    load_jac.start()

    barrier = pltpu.get_barrier_semaphore()
    for dp in sources:
        for to_cell in (cell, x_cell):
            if dp is me and to_cell is cell:
                continue
            pl.semaphore_signal(
                barrier, inc=1, device_id=(dp, to_cell), device_id_type=pl.DeviceIdType.MESH
            )

    @pl.loop(1, half)
    def _(k):
        pl.semaphore_signal(
            barrier, inc=1, device_id=(me, (line + k) % half * 2 + x),
            device_id_type=pl.DeviceIdType.MESH,
        )

    square = (tile, tile)

    def column(row):
        return jnp.transpose(jnp.broadcast_to(row, square))

    root = jnp.sqrt(weights[...])
    tq[0] = root * residual[...]
    wcol = column(root)[:, 0:1]
    tcol[0] = column(tq[0])
    v[...] = jnp.zeros_like(v)
    pl.semaphore_wait(barrier, 7 + half - 1)

    def half_of(ref, side):
        return ref.at[pl.ds(side * k_half, k_half)]

    def y_part(ref, p):
        return ref.at[pl.ds(core * k_half, k_half), :, pl.ds(p * LANES, LANES)]

    def y_copy(src, p, q):
        return remote(
            src, half_of(gy[p][q], core), y_s.at[p, q], y_r.at[p, q], y_peer, cell
        )

    def y_own(verb, p, q):
        pl.when(core == q)(lambda: each(verb, [y_copy(y_part(own_basis, p), p, q)]))

    def y_other(verb, p, q):
        pl.when(core != q)(lambda: each(verb, [y_copy(y_part(peer_basis, p), p, q)]))

    def swap(p, q, side):
        piece = half_of(gy[p][q], side)
        return remote(piece, piece, w_s.at[p, q], w_r.at[p, q], core_peer, cell)

    to_core = remote(own_basis, peer_basis, b_s.at[0], b_r.at[0], core_peer, cell)

    load_basis.wait()
    for q in range(2):
        y_own("start", order[0], q)
    to_core.start()

    t_targets = [
        (s, sources[(s // 4) * 2 + s % 2], x_cell if s // 2 % 2 else cell) for s in range(1, 8)
    ]
    t_copies = [
        remote(tq.at[0], tq.at[s], t_s.at[s], t_r.at[s], dp, to_cell)
        for s, dp, to_cell in t_targets
    ]
    each("start", t_copies)
    load_jac.wait()

    def lanes(n, dy=0, dc=0, sub=None):
        r, first, size = units[n]
        oy = 1 - y if dy else y
        oc = 1 - core if dc else core
        group = (oy * 2 + oc, oy * 2 + 1 - oc, (1 - oy) * 2, (1 - oy) * 2 + 1)[r]
        if sub is not None:
            first, size = first + sub[0], sub[1]
        return pl.ds(pl.multiple_of(group * width + first, LANES), size)

    def block_dot(n, b):
        r, first, size = units[n]
        for t in range(slot_count):
            held = (own_basis, peer_basis)[r] if r < 2 else gy[first // LANES][r - 2]
            rows = held[slots[b, t]]
            keep = jnp.minimum(jnp.maximum(live[b] - t, 0), 1).astype(f32)
            sel[t * tile:(t + 1) * tile, 0:size] = rows * keep.astype(rows.dtype)
        return jnp.dot(jac[b], sel[:, 0:size], preferred_element_type=f32)

    def part(refs, n, j):
        r, first, size = units[n]
        return [ref.at[r, j, :, first:first + size] for ref in refs]

    def x_copy(n, j):
        return pair(
            part((xq, xs), n, j), part((xrq, xrs), n, j), x_s, x_r, (n, j), (n, j), me, x_cell
        )

    def z_copy(n, j, slot):
        return pair(
            part((xrq, xrs), n, j), part((zrq, zrs), n, slot),
            z_s, z_r, (n, j), (n, slot), me, 2 * j + x,
        )

    def send_x(n):
        r, first, size = units[n]

        @pl.loop(0, half)
        def _(j):
            value, unit = code(block_dot(n, 2 * j + 1 - x))
            xq[r, j, :, first:first + size] = value
            xs[r, j, :, first:first + size] = unit
            each("start", x_copy(n, j))

    def send_z(n):
        r, first, size = units[n]
        cols = slice(first, first + size)

        def total(j):
            value = block_dot(n, 2 * j + x)
            each("wait_recv", x_copy(n, j))
            return value + decode(xrq[r, j, :, cols], xrs[r, j, :, cols])

        @pl.loop(1, half)
        def _(k):
            j = (line + k) % half
            value, unit = code(total(j))
            xrq[r, j, :, cols] = value
            xrs[r, j, :, cols] = unit
            each("start", z_copy(n, j, line))

        acc[r, :, cols] = total(line)

    def pass_on(p, q):
        y_copy(half_of(gy[p][q], core), p, q).wait_recv()
        swap(p, q, core).start()

    def held_columns(slot, n, at_x):
        r, first, size = units[n]
        sub, condition = None, None
        if aligned and slot // 2 % 2:
            if slot < 4 and r >= 2 and first != LANES:
                condition = first != 2 * LANES * (1 - at_x)
            if slot >= 4 and r < 2:
                sub = (at_x * LANES, 2 * LANES)
        return lanes(n, slot // 4, slot % 2, sub), condition

    def u_do(verb, n, slot):
        over_x = slot in (2, 6)
        source = SOURCE[slot]
        if verb == "wait_recv":
            cols, condition = held_columns(slot, n, x)
            source = slot
        else:
            at_x = 1 - x if over_x else x
            cols, _ = held_columns(source | 2 if over_x else source, n, at_x)
            _, condition = held_columns(slot, n, at_x)
        if over_x:
            dp, to_cell = me, x_cell
        else:
            dp, to_cell = (y_peer if slot == 4 else core_peer), cell

        def run():
            refs = [[ref.at[k, :, cols] for ref in (uq, us)] for k in (source, slot)]
            each(verb, pair(*refs, u_s, u_r, (slot, n), (slot, n), dp, to_cell))

        when(condition, run)

    def keep(slot, cols, value):
        high = value.astype(jnp.bfloat16)
        at = slice(slot * tile, (slot + 1) * tile)
        u[0, at, cols] = high
        u[1, at, cols] = (value - high.astype(f32)).astype(jnp.bfloat16)
        term = value * tcol[slot][:, 0:1]
        v[:, cols] = v[:, cols] + jnp.sum(term.reshape(tile // 8, 8, term.shape[1]), axis=0)

    def finish_rows(n):
        r, first, size = units[n]
        cols = slice(first, first + size)

        @pl.loop(1, half)
        def _(k):
            j = (line + k) % half
            each("wait_recv", z_copy(n, j, j))
            acc[r, :, cols] = acc[r, :, cols] + decode(
                zrq[r, j, :, cols], zrs[r, j, :, cols]
            )

        total = acc[r, :, cols]
        out = lanes(n)
        jq[:, out] = total
        scaled = total * wcol
        value, unit = code(scaled)
        uq[0, :, out] = value
        us[0, :, out] = unit
        for slot in (4, 2, 1):
            u_do("start", n, slot)
        keep(0, out, scaled)

    def relay_y(n):
        u_do("wait_recv", n, 4)
        u_do("start", n, 6)
        u_do("start", n, 5)

    def relay_x(n):
        u_do("wait_recv", n, 2)
        u_do("start", n, 3)

    def relay_xy(n):
        u_do("wait_recv", n, 6)
        u_do("start", n, 7)

    def take(n, slot):
        cols, condition = held_columns(slot, n, x)

        def run():
            keep(slot, cols, decode(uq[slot, :, cols], us[slot, :, cols]))

        when(condition, run)

    def take_core(n):
        u_do("wait_recv", n, 1)
        take(n, 1)

    def take_rest(n):
        for slot in (3, 5, 7):
            u_do("wait_recv", n, slot)
            take(n, slot)

    def take_relayed(n):
        for slot in (2, 4, 6):
            take(n, slot)

    count = len(units)
    send_x(0)
    to_core.wait_recv()
    for q in range(2):
        y_other("start", order[0], q)
    for p in order[1:]:
        for q in range(2):
            y_own("start", p, q)
            y_other("start", p, q)
    send_x(1)
    for q in range(2):
        pl.when(core == q)(lambda: pass_on(order[0], q))
    send_z(0)
    for q in range(2):
        pl.when(core != q)(lambda: pass_on(order[0], q))
    for c in t_copies:
        c.wait_recv()
    for s in range(1, 8):
        tcol[s] = column(tq[s])

    def arrived(n):
        swap(units[n][1] // LANES, units[n][0] - 2, 1 - core).wait_recv()

    def on(n):
        pass_on(units[n][1] // LANES, units[n][0] - 2)

    arrived(2)
    send_x(2)
    arrived(3)
    send_x(3)
    send_z(1)
    on(4)
    send_z(2)
    arrived(4)
    send_x(4)
    finish_rows(0)
    on(5)
    send_z(3)
    arrived(5)
    send_x(5)
    send_z(4)
    on(6)
    finish_rows(1)
    arrived(6)
    send_x(6)
    send_z(5)
    finish_rows(2)
    finish_rows(3)
    on(7)
    take_core(0)
    arrived(7)
    send_x(7)
    finish_rows(4)
    send_z(6)
    relay_y(0)
    relay_x(0)
    take_core(1)
    finish_rows(5)
    relay_y(1)
    relay_x(1)
    send_z(7)
    for n in range(2, 6):
        relay_y(n)
        relay_x(n)
    finish_rows(6)
    for n in range(0, 6):
        relay_xy(n)
        if n >= 2:
            take_core(n)
        take_relayed(n)
    finish_rows(7)
    for n in range(0, 6):
        take_rest(n)

    def row_start(j):
        return (2 * j + x) * own_rows

    def window_start(j):
        return jnp.minimum(row_start(j) // LANES * LANES, full - window)

    def g_copy(i, j, slot):
        gq, gs, grq, grs = gbufs[i]
        send, recv = g_sems[i]
        return pair(
            (gq.at[j], gs.at[j]), (grq.at[slot], grs.at[slot]), send, recv, (j,), (slot,),
            me, 2 * j + x,
        )

    def product(i, j):
        kind, size, columns, rows = chunks[i]
        if kind == "window":
            start, off = window_start(j), row_start(j) - window_start(j)
        elif kind == "outer":
            start, off = j * width + 2 * x * LANES, 0
        else:
            start, off = j * width + LANES, x * (LANES - rows)
        at = pl.ds(pl.multiple_of(start, LANES), size)
        done = 0
        for first, span in columns:
            right = pl.ds(pl.multiple_of(me * width + first, LANES), span)

            def dot(a, b):
                return lax.dot_general(
                    u[a, :, at], u[b, :, right], (((0,), (0,)), ((), ())),
                    preferred_element_type=f32,
                )

            prod[0:size, done:done + span] = (
                dot(0, 0) + (dot(0, 1) + dot(1, 0))
            ) / ndata
            done += span
        if kind == "outer":
            return prod[0:rows, 0:done]
        return prod[pl.ds(pl.multiple_of(off, 8), rows), 0:done]

    def own_place(i):
        kind, size, columns, rows = chunks[i]
        at = {"window": 0, "outer": x * (own_rows - rows), "inner": (1 - x) * (own_rows - rows)}[kind]
        return pl.ds(at if kind == "window" else pl.multiple_of(at, 8), rows)

    def gram(i):
        @pl.loop(1, half)
        def _(k):
            j = (line + k) % half
            gq, gs, _, _ = gbufs[i]
            gq[j], gs[j] = code(product(i, j))
            each("start", g_copy(i, j, line))

    def gram_own(i):
        value, done = product(i, line), 0
        for first, span in chunks[i][2]:
            sysb[own_place(i), first:first + span] = value[:, done:done + span]
            done += span

    def gram_add(i):
        @pl.loop(1, half)
        def _(k):
            j = (line + k) % half
            each("wait_recv", g_copy(i, j, j))
            _, _, grq, grs = gbufs[i]
            done = 0
            for first, span in chunks[i][2]:
                at = (own_place(i), slice(first, first + span))
                part = slice(done, done + span)
                sysb[at] = sysb[at] + decode(grq[j, :, part], grs[j, :, part])
                done += span

    def vz_copy(j, slot):
        at = pl.ds(pl.multiple_of(window_start(j), LANES), window)
        return remote(v.at[:, at], vr.at[slot], vz_s.at[j], vz_r.at[slot], me, 2 * j + x)

    late = range(6, count)
    if aligned:
        gram(0)
        for n in late:
            relay_y(n)
            relay_x(n)
        gram_own(0)
    else:
        for n in late:
            relay_y(n)
            relay_x(n)
    for n in late:
        take_core(n)
        relay_xy(n)
        take_relayed(n)
    for n in late:
        take_rest(n)

    rest = range(1 if aligned else 0, len(chunks))
    for i in rest:
        gram(i)

    @pl.loop(1, half)
    def _(k):
        vz_copy((line + k) % half, line).start()

    for i in rest:
        gram_own(i)
    for i in range(len(chunks)):
        gram_add(i)

    def s_copy(i, src, dst, dp):
        return pair(
            (sq.at[src], su.at[src]), (sq.at[dst], su.at[dst]), s_s, s_r, (i,), (i,), dp, cell
        )

    sq[0], su[0] = code(sysb[...])
    s_y, s_core, s_on = s_copy(1, 0, 2, y_peer), s_copy(0, 0, 1, core_peer), s_copy(2, 2, 3, core_peer)
    each("start", s_y)
    each("start", s_core)

    vr[line] = v[:, pl.ds(pl.multiple_of(window_start(line), LANES), window)]
    total = vr[line]
    for k in range(1, half):
        j = (line + k) % half
        vz_copy(j, j).wait_recv()
        total = total + vr[j]
    misfit = jnp.sum(total, axis=0, keepdims=True) / math.sqrt(ndata)
    offset = row_start(line) - window_start(line)
    own = jnp.zeros(rhs.shape, f32)
    starts = [c * own_rows for c in range(n_cells)]
    for off in sorted({s - min(s // LANES * LANES, full - window) for s in starts}):
        own = jnp.where(offset == off, misfit[:, off:off + own_rows], own)
    rhs[...] = own

    def finish(r):
        shape = (own_rows, width)
        row = lax.broadcasted_iota(jnp.int32, shape, 0) + cell * own_rows
        col = lax.broadcasted_iota(jnp.int32, shape, 1) + sources[r] * width
        at = pl.ds(pl.multiple_of(sources[r] * width, LANES), width)
        system[:, at] = decode(sq[r], su[r]) + (row == col).astype(f32)

    finish(0)
    each("wait_recv", s_core)
    finish(1)
    each("wait_recv", s_y)
    each("start", s_on)
    finish(2)
    each("wait_recv", s_on)
    finish(3)

    to_core.wait_send()
    for p in order:
        for q in range(2):
            y_own("wait_send", p, q)
            y_other("wait_send", p, q)
            swap(p, q, core).wait_send()
    for n in range(count):
        for slot in range(1, 8):
            u_do("wait_send", n, slot)
    each("wait_send", t_copies + s_y + s_core + s_on)

    @pl.loop(0, half)
    def _(j):
        for n in range(count):
            each("wait_send", x_copy(n, j))

    @pl.loop(1, half)
    def _(k):
        j = (line + k) % half
        for n in range(count):
            each("wait_send", z_copy(n, j, line))
        for i in range(len(chunks)):
            each("wait_send", g_copy(i, j, line))
        vz_copy(j, line).wait_send()


def on_device(jac_blocks, slot_cell_blocks, live_counts, eigen_basis, weights, residual):
    n_cells = lax.axis_size("cells")
    n_groups = lax.axis_size("dp")
    half = n_cells // 2
    tile = jac_blocks.shape[1]
    depth, width = eigen_basis.shape
    full = width * n_groups
    rows_here = full // n_cells
    ndata = weights.shape[0] * n_cells * n_groups
    pieces = width // LANES
    assert n_groups == 4 and n_cells % 2 == 0 and pieces == 3
    assert jac_blocks.shape[0] == n_cells and weights.shape[0] == tile
    aligned = 2 * rows_here == width
    order = (0, 2, 1)
    units = [(0, 0, width), (1, 0, width)]
    for p in order:
        units += [(2, p * LANES, LANES), (3, p * LANES, LANES)]
    window = 2 * LANES
    if aligned:
        outer = ((0, LANES), (2 * LANES, LANES))
        chunks = (
            ("outer", LANES, outer, LANES),
            ("window", window, ((LANES, LANES),), rows_here),
            ("inner", LANES, outer, rows_here - LANES),
        )
    else:
        chunks = (("window", window, ((0, width),), rows_here),)
    f32, bf16, i16 = jnp.float32, jnp.bfloat16, jnp.int16
    vmem, smem, anywhere = (
        pl.BlockSpec(memory_space=s) for s in (pltpu.VMEM, pltpu.SMEM, pl.ANY)
    )

    def sems(*shape):
        return [pltpu.SemaphoreType.DMA(shape)] * 2

    def coded(*lead, rows, columns):
        return [pltpu.VMEM((*lead, rows, columns), i16), pltpu.VMEM((*lead, 1, columns), f32)]

    gbufs = tuple(
        tuple(coded(half, rows=rows, columns=sum(c[1] for c in columns)) * 2)
        for _, _, columns, rows in chunks
    )
    blocks = depth // tile
    jq, system, rhs = pl.pallas_call(
        functools.partial(fused, n_cells, ndata, tuple(units), order, chunks, aligned),
        out_shape=(
            jax.ShapeDtypeStruct((tile, full), f32),
            jax.ShapeDtypeStruct((rows_here, full), f32),
            jax.ShapeDtypeStruct((1, rows_here), f32),
        ),
        in_specs=[smem, smem, anywhere, anywhere, vmem, vmem],
        out_specs=(vmem, vmem, vmem),
        scratch_shapes=[
            pltpu.VMEM((blocks, tile, width), bf16),
            pltpu.VMEM((blocks, tile, width), bf16),
            ((pltpu.VMEM((blocks, tile, LANES), bf16),) * 2,) * pieces,
            pltpu.VMEM(jac_blocks.shape, bf16),
            pltpu.VMEM((jac_blocks.shape[2], width), bf16),
            *coded(4, half, rows=tile, columns=width),
            *coded(4, half, rows=tile, columns=width),
            *coded(4, half, rows=tile, columns=width),
            pltpu.VMEM((4, tile, width), f32),
            *coded(8, rows=tile, columns=full),
            pltpu.VMEM((2, 8 * tile, full), bf16),
            pltpu.VMEM((8, full), f32),
            pltpu.VMEM((8, 1, tile), f32),
            pltpu.VMEM((8, tile, tile), f32),
            pltpu.VMEM((window, width), f32),
            gbufs,
            pltpu.VMEM((rows_here, width), f32),
            pltpu.VMEM((half, 8, window), f32),
            *coded(4, rows=rows_here, columns=width),
            pltpu.SemaphoreType.DMA((2,)),
            *sems(1), *sems(pieces, 2), *sems(pieces, 2),
            *sems(2, len(units), half), *sems(2, len(units), half),
            *sems(2, 8, len(units)), *sems(8), *sems(half), *sems(2, 3),
            tuple(tuple(sems(2, half)) for _ in chunks),
        ],
        compiler_params=pltpu.CompilerParams(
            collective_id=0, has_side_effects=True, vmem_limit_bytes=60 * 1024 * 1024
        ),
    )(
        slot_cell_blocks, live_counts[:, 0], jac_blocks,
        eigen_basis.reshape(blocks, tile, width), weights[None], residual[None],
    )
    return jq, system, rhs[0]


def solution(mesh):
    placed = (
        P("dp", None, "cells"),
        P("dp", "cells"),
        P("dp", "cells"),
        P("cells", "dp"),
        P(("dp", "cells")),
        P(("dp", "cells")),
    )
    return jax.shard_map(
        on_device,
        mesh=mesh,
        in_specs=placed,
        out_specs=(P(("dp", "cells"), None), P("cells", None), P("cells")),
        check_vma=False,
    )
```

```python
import functools
import math

import jax
import jax.numpy as jnp
from jax import lax
from jax.experimental import pallas as pl
from jax.experimental.pallas import tpu as pltpu
from jax.sharding import PartitionSpec as P

LANES = 128
SOURCE = {1: 0, 2: 0, 4: 0, 6: 4, 3: 2, 5: 4, 7: 6}


def code(value):
    top = jnp.maximum(jnp.max(jnp.abs(value), axis=0, keepdims=True), 1e-30)
    whole = jnp.round(value * (32767.0 / top))
    return whole.astype(jnp.int32).astype(jnp.int16), top * (1.0 / 32767.0)


def decode(whole, unit):
    return whole.astype(jnp.int32).astype(jnp.float32) * unit


def fused(
    n_cells, ndata, units, order, chunks, aligned,
    slots, live, jac_in, basis_in, weights, residual,
    jq, system, rhs,
    own_basis, peer_basis, gy, jac, xq, xs, xrq, xrs, zrq, zrs, acc, uq, us, ut, right, v,
    tq, tcol, gbufs, sysb, vr, sq, su,
    in_s, b_s, b_r, y_s, y_r, w_s, w_r, x_s, x_r, z_s, z_r, u_s, u_r, t_s, t_r,
    vz_s, vz_r, s_s, s_r, g_sems,
):
    f32 = jnp.float32
    half = n_cells // 2
    tile = jac.shape[1]
    slot_count = jac.shape[2] // tile
    width = basis_in.shape[2]
    full = uq.shape[2]
    own_rows = sysb.shape[0]
    k_half = own_basis.shape[0] // 2
    window = vr.shape[2]
    me, cell = lax.axis_index("dp"), lax.axis_index("cells")
    core, y = me % 2, me // 2
    core_peer = y * 2 + 1 - core
    y_peer = (1 - y) * 2 + core
    far_peer = (1 - y) * 2 + 1 - core
    sources = (me, core_peer, y_peer, far_peer)
    x, line = cell % 2, cell // 2
    x_cell = line * 2 + 1 - x

    def remote(src, dst, send, recv, dp, to_cell):
        return pltpu.make_async_remote_copy(
            src_ref=src, dst_ref=dst, send_sem=send, recv_sem=recv,
            device_id=(dp, to_cell), device_id_type=pl.DeviceIdType.MESH,
        )

    def pair(src, dst, send, recv, at, to, dp, to_cell):
        return [
            remote(src[i], dst[i], send.at[(i, *at)], recv.at[(i, *to)], dp, to_cell)
            for i in range(2)
        ]

    def each(verb, copies):
        for copy in copies:
            getattr(copy, verb)()

    def when(condition, run):
        if condition is None:
            run()
        else:
            pl.when(condition)(run)

    load_basis = pltpu.make_async_copy(basis_in, own_basis, in_s.at[0])
    load_jac = pltpu.make_async_copy(jac_in, jac, in_s.at[1])
    load_basis.start()
    load_jac.start()

    barrier = pltpu.get_barrier_semaphore()
    for dp in sources:
        for to_cell in (cell, x_cell):
            if dp is me and to_cell is cell:
                continue
            pl.semaphore_signal(
                barrier, inc=1, device_id=(dp, to_cell), device_id_type=pl.DeviceIdType.MESH
            )

    @pl.loop(1, half)
    def _(k):
        pl.semaphore_signal(
            barrier, inc=1, device_id=(me, (line + k) % half * 2 + x),
            device_id_type=pl.DeviceIdType.MESH,
        )

    square = (tile, tile)

    def column(row):
        return jnp.transpose(jnp.broadcast_to(row, square))

    root = jnp.sqrt(weights[...])
    tq[0] = root * residual[...]
    wcol = column(root)[:, 0:1]
    tcol[0] = column(tq[0])
    v[...] = jnp.zeros_like(v)
    pl.semaphore_wait(barrier, 7 + half - 1)

    def half_of(ref, side):
        return ref.at[pl.ds(side * k_half, k_half)]

    def y_part(ref, p):
        return ref.at[pl.ds(core * k_half, k_half), :, pl.ds(p * LANES, LANES)]

    def y_copy(src, p, q):
        return remote(
            src, half_of(gy[p][q], core), y_s.at[p, q], y_r.at[p, q], y_peer, cell
        )

    def y_own(verb, p, q):
        pl.when(core == q)(lambda: each(verb, [y_copy(y_part(own_basis, p), p, q)]))

    def y_other(verb, p, q):
        pl.when(core != q)(lambda: each(verb, [y_copy(y_part(peer_basis, p), p, q)]))

    def swap(p, q, side):
        piece = half_of(gy[p][q], side)
        return remote(piece, piece, w_s.at[p, q], w_r.at[p, q], core_peer, cell)

    to_core = remote(own_basis, peer_basis, b_s.at[0], b_r.at[0], core_peer, cell)

    load_basis.wait()
    for q in range(2):
        y_own("start", order[0], q)
    to_core.start()

    t_targets = [
        (s, sources[(s // 4) * 2 + s % 2], x_cell if s // 2 % 2 else cell) for s in range(1, 8)
    ]
    t_copies = [
        remote(tq.at[0], tq.at[s], t_s.at[s], t_r.at[s], dp, to_cell)
        for s, dp, to_cell in t_targets
    ]
    each("start", t_copies)
    load_jac.wait()

    def lanes(n, dy=0, dc=0, sub=None):
        r, first, size = units[n]
        oy = 1 - y if dy else y
        oc = 1 - core if dc else core
        group = (oy * 2 + oc, oy * 2 + 1 - oc, (1 - oy) * 2, (1 - oy) * 2 + 1)[r]
        if sub is not None:
            first, size = first + sub[0], sub[1]
        return pl.ds(pl.multiple_of(group * width + first, LANES), size)

    def block_dot(n, b):
        r, first, size = units[n]
        held = (own_basis, peer_basis)[r] if r < 2 else gy[first // LANES][r - 2]
        if n == 0:
            for t in range(slot_count):
                at = slice(t * tile, (t + 1) * tile)
                keep = jnp.minimum(jnp.maximum(live[b] - t, 0), 1).astype(f32)
                jac[b, :, at] = jac[b, :, at] * keep.astype(jac.dtype)
        rows = [held[slots[b, t]] for t in range(slot_count)]
        return jnp.dot(jac[b], jnp.concatenate(rows, axis=0), preferred_element_type=f32)

    def part(refs, n, j):
        r, first, size = units[n]
        return [ref.at[r, j, :, first:first + size] for ref in refs]

    def x_copy(n, j):
        return pair(
            part((xq, xs), n, j), part((xrq, xrs), n, j), x_s, x_r, (n, j), (n, j), me, x_cell
        )

    def z_copy(n, j, slot):
        return pair(
            part((xrq, xrs), n, j), part((zrq, zrs), n, slot),
            z_s, z_r, (n, j), (n, slot), me, 2 * j + x,
        )

    def send_x(n):
        r, first, size = units[n]

        @pl.loop(0, half, unroll=4)
        def _(j):
            value, unit = code(block_dot(n, 2 * j + 1 - x))
            xq[r, j, :, first:first + size] = value
            xs[r, j, :, first:first + size] = unit
            each("start", x_copy(n, j))

    def send_z(n):
        r, first, size = units[n]
        cols = slice(first, first + size)

        def total(j):
            value = block_dot(n, 2 * j + x)
            each("wait_recv", x_copy(n, j))
            return value + decode(xrq[r, j, :, cols], xrs[r, j, :, cols])

        @pl.loop(1, half, unroll=3)
        def _(k):
            j = (line + k) % half
            value, unit = code(total(j))
            xrq[r, j, :, cols] = value
            xrs[r, j, :, cols] = unit
            each("start", z_copy(n, j, line))

        acc[r, :, cols] = total(line)

    def pass_on(p, q):
        y_copy(half_of(gy[p][q], core), p, q).wait_recv()
        swap(p, q, core).start()

    count = len(units)
    late = range(6, count)

    def held_columns(slot, n, at_x):
        r, first, size = units[n]
        sub, condition = None, None
        if aligned and slot // 2 % 2:
            if slot < 4 and r >= 2 and first != LANES:
                condition = first != 2 * LANES * (1 - at_x)
            if slot >= 4 and r < 2:
                sub = (at_x * LANES, 2 * LANES)
        return lanes(n, slot // 4, slot % 2, sub), condition

    def u_do(verb, n, slot):
        over_x = slot in (2, 6)
        direct = slot == 6 and n in late
        source = 0 if direct else SOURCE[slot]
        if verb == "wait_recv":
            cols, condition = held_columns(slot, n, x)
            source = slot
        else:
            at_x = 1 - x if over_x else x
            assert not (direct and units[n][0] < 2)
            cols, _ = held_columns(source | 2 if over_x else source, n, at_x)
            _, condition = held_columns(slot, n, at_x)
        if over_x:
            dp, to_cell = (y_peer if direct else me), x_cell
        else:
            dp, to_cell = (y_peer if slot == 4 else core_peer), cell

        def run():
            refs = [[ref.at[k, :, cols] for ref in (uq, us)] for k in (source, slot)]
            each(verb, pair(*refs, u_s, u_r, (slot, n), (slot, n), dp, to_cell))

        when(condition, run)

    place = {p: i * LANES for i, p in enumerate(order)}

    def turn(slot, first, size):
        cols = pl.ds(pl.multiple_of(first, LANES), size)
        value = decode(uq[slot, :, cols], us[slot, :, cols])
        term = value * tcol[slot][:, 0:1]
        v[:, cols] = v[:, cols] + jnp.sum(term.reshape(tile // 8, 8, size), axis=0)
        turned = jnp.transpose(value)
        high = turned.astype(jnp.bfloat16)
        at = slice(slot * tile, (slot + 1) * tile)
        ut[cols, at] = high
        at = slice((8 + slot) * tile, (9 + slot) * tile)
        ut[cols, at] = (turned - high.astype(f32)).astype(jnp.bfloat16)

    def own_columns(slot, p):
        cols = pl.ds(pl.multiple_of(me * width + p * LANES, LANES), LANES)
        value = decode(uq[slot, :, cols], us[slot, :, cols])
        high = value.astype(jnp.bfloat16)
        at = slice(place[p], place[p] + LANES)
        for k in (slot, 8 + slot):
            right[k * tile:(k + 1) * tile, at] = high
        right[(16 + slot) * tile:(17 + slot) * tile, at] = (
            value - high.astype(f32)
        ).astype(jnp.bfloat16)

    def take(n, slot):
        r, first, size = units[n]
        dy, dc = slot // 4, slot % 2
        oy, oc = (1 - y if dy else y), (1 - core if dc else core)
        start = (oy * 2 + oc, oy * 2 + 1 - oc, (1 - oy) * 2, (1 - oy) * 2 + 1)[r] * width + first
        if not aligned:
            turn(slot, start, size)
        elif r < 2:
            turn(slot, start + x * LANES, 2 * LANES)
        elif first == LANES:
            turn(slot, start, size)
        else:
            pl.when(first == 2 * LANES * x)(lambda: turn(slot, start, size))
        if r < 2 and not dy and r == dc:
            for p in order:
                own_columns(slot, p)
        if r >= 2 and dy:
            pl.when(core == r - 2)(lambda: own_columns(slot, first // LANES))

    def finish_rows(n):
        r, first, size = units[n]
        cols = slice(first, first + size)

        @pl.loop(1, half, unroll=3)
        def _(k):
            j = (line + k) % half
            each("wait_recv", z_copy(n, j, j))
            acc[r, :, cols] = acc[r, :, cols] + decode(
                zrq[r, j, :, cols], zrs[r, j, :, cols]
            )

        total = acc[r, :, cols]
        out = lanes(n)
        jq[:, out] = total
        scaled = total * wcol
        value, unit = code(scaled)
        uq[0, :, out] = value
        us[0, :, out] = unit
        for slot in (4, 2, 1):
            u_do("start", n, slot)
        if n in late:
            u_do("start", n, 6)

    def relay_y(n):
        u_do("wait_recv", n, 4)
        if n not in late:
            u_do("start", n, 6)
        u_do("start", n, 5)

    def relay_x(n):
        u_do("wait_recv", n, 2)
        u_do("start", n, 3)

    def relay_xy(n):
        u_do("wait_recv", n, 6)
        u_do("start", n, 7)

    def take_core(n):
        u_do("wait_recv", n, 1)
        take(n, 1)

    def take_rest(n):
        for slot in (3, 5, 7):
            u_do("wait_recv", n, slot)
            take(n, slot)

    def take_relayed(n):
        for slot in (2, 4, 6):
            take(n, slot)

    send_x(0)
    to_core.wait_recv()
    for q in range(2):
        y_other("start", order[0], q)
    for p in order[1:]:
        for q in range(2):
            y_own("start", p, q)
            y_other("start", p, q)
    send_x(1)
    for q in range(2):
        pl.when(core == q)(lambda: pass_on(order[0], q))
    send_z(0)
    for q in range(2):
        pl.when(core != q)(lambda: pass_on(order[0], q))
    for c in t_copies:
        c.wait_recv()
    for s in range(1, 8):
        tcol[s] = column(tq[s])

    def arrived(n):
        swap(units[n][1] // LANES, units[n][0] - 2, 1 - core).wait_recv()

    def on(n):
        pass_on(units[n][1] // LANES, units[n][0] - 2)

    arrived(2)
    send_x(2)
    arrived(3)
    send_x(3)
    send_z(1)
    on(4)
    send_z(2)
    arrived(4)
    send_x(4)
    finish_rows(0)
    on(5)
    send_z(3)
    arrived(5)
    send_x(5)
    send_z(4)
    on(6)
    finish_rows(1)
    arrived(6)
    send_x(6)
    send_z(5)
    finish_rows(2)
    finish_rows(3)
    on(7)
    take_core(0)
    arrived(7)
    send_x(7)
    finish_rows(4)
    send_z(6)
    relay_y(0)
    relay_x(0)
    take_core(1)
    finish_rows(5)
    relay_y(1)
    relay_x(1)
    send_z(7)
    for n in range(2, 6):
        relay_y(n)
        relay_x(n)
    finish_rows(6)
    for n in range(0, 6):
        relay_xy(n)
        take(n, 0)
        if n >= 2:
            take_core(n)
        take_relayed(n)
    finish_rows(7)
    for n in range(0, 6):
        take_rest(n)

    def row_start(j):
        return (2 * j + x) * own_rows

    def window_start(j):
        return jnp.minimum(row_start(j) // LANES * LANES, full - window)

    def g_copy(i, j, slot):
        gq, gs, grq, grs = gbufs[i][1:]
        send, recv = g_sems[i]
        return pair(
            (gq.at[j], gs.at[j]), (grq.at[slot], grs.at[slot]), send, recv, (j,), (slot,),
            me, 2 * j + x,
        )

    def product(i):
        kind, first, size, rows = chunks[i]
        starts = [
            {"outer": j * width + 2 * x * LANES, "inner": j * width + LANES + x * rows,
             "all": row_start(j)}[kind] for j in range(half)
        ]

        def left(depth):
            return jnp.concatenate(
                [ut[pl.ds(pl.multiple_of(start, 16), rows), 0:depth] for start in starts], axis=0
            )

        at, deep = slice(first, first + size), 8 * tile
        value = jnp.dot(left(2 * deep), right[0:2 * deep, at], preferred_element_type=f32)
        value = value + jnp.dot(left(deep), right[2 * deep:, at], preferred_element_type=f32)
        gbufs[i][0][...] = value.reshape(half, rows, size)

    def own_place(i):
        kind, _, _, rows = chunks[i]
        if kind == "all":
            return pl.ds(0, rows)
        at = (x if kind == "outer" else 1 - x) * (own_rows - rows)
        return pl.ds(pl.multiple_of(at, 8), rows)

    def spans(i):
        _, first, size, _ = chunks[i]
        for p in order:
            if first <= place[p] < first + size:
                at = place[p] - first
                yield slice(p * LANES, (p + 1) * LANES), slice(at, at + LANES)

    def gram(i):
        product(i)

        @pl.loop(1, half, unroll=3)
        def _(k):
            j = (line + k) % half
            gq, gs = gbufs[i][1:3]
            value, unit = code(gbufs[i][0][j])
            gq[j] = value
            gs[j] = unit * (1.0 / ndata)
            each("start", g_copy(i, j, line))

    def gram_own(i):
        for to, part in spans(i):
            sysb[own_place(i), to] = gbufs[i][0][line, :, part] * (1.0 / ndata)

    def gram_add(i):
        @pl.loop(1, half, unroll=3)
        def _(k):
            j = (line + k) % half
            each("wait_recv", g_copy(i, j, j))
            grq, grs = gbufs[i][3:]
            for to, part in spans(i):
                at = (own_place(i), to)
                sysb[at] = sysb[at] + decode(grq[j, :, part], grs[j, :, part])

    def vz_copy(j, slot):
        at = pl.ds(pl.multiple_of(window_start(j), LANES), window)
        return remote(v.at[:, at], vr.at[slot], vz_s.at[j], vz_r.at[slot], me, 2 * j + x)

    for n in late[:1]:
        relay_y(n)
        relay_x(n)
        relay_xy(n)
    if aligned:
        gram(0)
    for n in late[1:]:
        relay_y(n)
        relay_x(n)
        relay_xy(n)
    if aligned:
        gram_own(0)
    for n in late:
        take(n, 0)
        take_core(n)
        take_relayed(n)
    for n in late:
        take_rest(n)

    rest = range(1 if aligned else 0, len(chunks))
    for i in rest:
        gram(i)

    @pl.loop(1, half, unroll=3)
    def _(k):
        vz_copy((line + k) % half, line).start()

    for i in rest:
        gram_own(i)
    for i in range(len(chunks)):
        gram_add(i)

    def s_copy(i, src, dst, dp):
        return pair(
            (sq.at[src], su.at[src]), (sq.at[dst], su.at[dst]), s_s, s_r, (i,), (i,), dp, cell
        )

    sq[0], su[0] = code(sysb[...])
    s_y, s_core, s_on = s_copy(1, 0, 2, y_peer), s_copy(0, 0, 1, core_peer), s_copy(2, 2, 3, core_peer)
    each("start", s_y)
    each("start", s_core)

    vr[line] = v[:, pl.ds(pl.multiple_of(window_start(line), LANES), window)]
    total = vr[line]
    for k in range(1, half):
        j = (line + k) % half
        vz_copy(j, j).wait_recv()
        total = total + vr[j]
    misfit = jnp.sum(total, axis=0, keepdims=True) / math.sqrt(ndata)
    offset = row_start(line) - window_start(line)
    own = jnp.zeros(rhs.shape, f32)
    starts = [c * own_rows for c in range(n_cells)]
    for off in sorted({s - min(s // LANES * LANES, full - window) for s in starts}):
        own = jnp.where(offset == off, misfit[:, off:off + own_rows], own)
    rhs[...] = own

    def finish(r):
        shape = (own_rows, width)
        row = lax.broadcasted_iota(jnp.int32, shape, 0) + cell * own_rows
        col = lax.broadcasted_iota(jnp.int32, shape, 1) + sources[r] * width
        at = pl.ds(pl.multiple_of(sources[r] * width, LANES), width)
        system[:, at] = decode(sq[r], su[r]) + (row == col).astype(f32)

    finish(0)
    each("wait_recv", s_core)
    finish(1)
    each("wait_recv", s_y)
    each("start", s_on)
    finish(2)
    each("wait_recv", s_on)
    finish(3)

    to_core.wait_send()
    for p in order:
        for q in range(2):
            y_own("wait_send", p, q)
            y_other("wait_send", p, q)
            swap(p, q, core).wait_send()
    for n in range(count):
        for slot in range(1, 8):
            u_do("wait_send", n, slot)
    each("wait_send", t_copies + s_y + s_core + s_on)

    @pl.loop(0, half)
    def _(j):
        for n in range(count):
            each("wait_send", x_copy(n, j))

    @pl.loop(1, half)
    def _(k):
        j = (line + k) % half
        for n in range(count):
            each("wait_send", z_copy(n, j, line))
        for i in range(len(chunks)):
            each("wait_send", g_copy(i, j, line))
        vz_copy(j, line).wait_send()


def on_device(jac_blocks, slot_cell_blocks, live_counts, eigen_basis, weights, residual):
    n_cells = lax.axis_size("cells")
    n_groups = lax.axis_size("dp")
    half = n_cells // 2
    tile = jac_blocks.shape[1]
    depth, width = eigen_basis.shape
    full = width * n_groups
    rows_here = full // n_cells
    ndata = weights.shape[0] * n_cells * n_groups
    pieces = width // LANES
    assert n_groups == 4 and n_cells % 2 == 0 and pieces == 3
    assert jac_blocks.shape[0] == n_cells and weights.shape[0] == tile
    aligned = 2 * rows_here == width
    order = (0, 2, 1)
    units = [(0, 0, width), (1, 0, width)]
    for p in order:
        units += [(2, p * LANES, LANES), (3, p * LANES, LANES)]
    window = 2 * LANES
    if aligned:
        chunks = (
            ("outer", 0, 2 * LANES, LANES),
            ("outer", 2 * LANES, LANES, LANES),
            ("inner", 0, width, rows_here - LANES),
        )
    else:
        chunks = (("all", 0, width, rows_here),)
    f32, bf16, i16 = jnp.float32, jnp.bfloat16, jnp.int16
    vmem, smem, anywhere = (
        pl.BlockSpec(memory_space=s) for s in (pltpu.VMEM, pltpu.SMEM, pl.ANY)
    )

    def sems(*shape):
        return [pltpu.SemaphoreType.DMA(shape)] * 2

    def coded(*lead, rows, columns):
        return [pltpu.VMEM((*lead, rows, columns), i16), pltpu.VMEM((*lead, 1, columns), f32)]

    gbufs = tuple(
        (pltpu.VMEM((half, rows, size), f32), *(coded(half, rows=rows, columns=size) * 2))
        for _, _, size, rows in chunks
    )
    blocks = depth // tile
    jq, system, rhs = pl.pallas_call(
        functools.partial(fused, n_cells, ndata, tuple(units), order, chunks, aligned),
        out_shape=(
            jax.ShapeDtypeStruct((tile, full), f32),
            jax.ShapeDtypeStruct((rows_here, full), f32),
            jax.ShapeDtypeStruct((1, rows_here), f32),
        ),
        in_specs=[smem, smem, anywhere, anywhere, vmem, vmem],
        out_specs=(vmem, vmem, vmem),
        scratch_shapes=[
            pltpu.VMEM((blocks, tile, width), bf16),
            pltpu.VMEM((blocks, tile, width), bf16),
            ((pltpu.VMEM((blocks, tile, LANES), bf16),) * 2,) * pieces,
            pltpu.VMEM(jac_blocks.shape, bf16),
            *coded(4, half, rows=tile, columns=width),
            *coded(4, half, rows=tile, columns=width),
            *coded(4, half, rows=tile, columns=width),
            pltpu.VMEM((4, tile, width), f32),
            *coded(8, rows=tile, columns=full),
            pltpu.VMEM((full, 16 * tile), bf16),
            pltpu.VMEM((24 * tile, width), bf16),
            pltpu.VMEM((8, full), f32),
            pltpu.VMEM((8, 1, tile), f32),
            pltpu.VMEM((8, tile, tile), f32),
            gbufs,
            pltpu.VMEM((rows_here, width), f32),
            pltpu.VMEM((half, 8, window), f32),
            *coded(4, rows=rows_here, columns=width),
            pltpu.SemaphoreType.DMA((2,)),
            *sems(1), *sems(pieces, 2), *sems(pieces, 2),
            *sems(2, len(units), half), *sems(2, len(units), half),
            *sems(2, 8, len(units)), *sems(8), *sems(half), *sems(2, 3),
            tuple(tuple(sems(2, half)) for _ in chunks),
        ],
        compiler_params=pltpu.CompilerParams(
            collective_id=0, has_side_effects=True, vmem_limit_bytes=60 * 1024 * 1024
        ),
    )(
        slot_cell_blocks, live_counts[:, 0], jac_blocks,
        eigen_basis.reshape(blocks, tile, width), weights[None], residual[None],
    )
    return jq, system, rhs[0]


def solution(mesh):
    placed = (
        P("dp", None, "cells"),
        P("dp", "cells"),
        P("dp", "cells"),
        P("cells", "dp"),
        P(("dp", "cells")),
        P(("dp", "cells")),
    )
    return jax.shard_map(
        on_device,
        mesh=mesh,
        in_specs=placed,
        out_specs=(P(("dp", "cells"), None), P("cells", None), P("cells")),
        check_vma=False,
    )
```

```python
import functools
import math

import jax
import jax.numpy as jnp
from jax import lax
from jax.experimental import pallas as pl
from jax.experimental.pallas import tpu as pltpu
from jax.sharding import PartitionSpec as P

LANES = 128
SOURCE = {1: 0, 2: 0, 4: 0, 3: 2, 5: 4, 7: 6}


def code(value):
    top = jnp.maximum(jnp.max(jnp.abs(value), axis=0, keepdims=True), 1e-30)
    whole = jnp.round(value * (32767.0 / top))
    return whole.astype(jnp.int32).astype(jnp.int16), top * (1.0 / 32767.0)


def decode(whole, unit):
    return whole.astype(jnp.int32).astype(jnp.float32) * unit


def fused(
    n_cells, ndata, units, order, chunks, aligned,
    slots_in, live_in, jac_in, basis_in, weights_in, residual_in,
    jq_out, system_out, rhs_out,
    slots, live, weights, residual, jq, system, rhs,
    own_basis, peer_basis, gy, jac, xq, xs, xrq, xrs, zrq, zrs, acc, uq, us, ut, right, v,
    tq, tcol, gbufs, sbufs, vr,
    in_s, b_s, b_r, y_s, y_r, w_s, w_r, x_s, x_r, z_s, z_r, u_s, u_r, t_s, t_r,
    vz_s, vz_r, g_sems, s_sems,
):
    f32 = jnp.float32
    half = n_cells // 2
    tile = jac.shape[1]
    slot_count = jac.shape[2] // tile
    width = basis_in.shape[2]
    full = uq.shape[2]
    own_rows = system.shape[0]
    k_half = own_basis.shape[0] // 2
    window = vr.shape[2]
    me, cell = lax.axis_index("dp"), lax.axis_index("cells")
    core, y = me % 2, me // 2
    core_peer = y * 2 + 1 - core
    y_peer = (1 - y) * 2 + core
    far_peer = (1 - y) * 2 + 1 - core
    sources = (me, core_peer, y_peer, far_peer)
    x, line = cell % 2, cell // 2
    x_cell = line * 2 + 1 - x

    def remote(src, dst, send, recv, dp, to_cell):
        return pltpu.make_async_remote_copy(
            src_ref=src, dst_ref=dst, send_sem=send, recv_sem=recv,
            device_id=(dp, to_cell), device_id_type=pl.DeviceIdType.MESH,
        )

    def pair(src, dst, send, recv, at, to, dp, to_cell):
        return [
            remote(src[i], dst[i], send.at[(i, *at)], recv.at[(i, *to)], dp, to_cell)
            for i in range(2)
        ]

    def each(verb, copies):
        for copy in copies:
            getattr(copy, verb)()

    def when(condition, run):
        if condition is None:
            run()
        else:
            pl.when(condition)(run)

    load_basis = pltpu.make_async_copy(basis_in, own_basis, in_s.at[0])
    load_jac = pltpu.make_async_copy(jac_in, jac, in_s.at[1])
    load_basis.start()
    small = [
        pltpu.make_async_copy(src, dst, in_s.at[2 + i])
        for i, (src, dst) in enumerate((
            (weights_in, weights), (residual_in, residual), (slots_in, slots), (live_in, live)
        ))
    ]
    each("start", small)
    load_jac.start()

    barrier = pltpu.get_barrier_semaphore()
    for dp in sources:
        for to_cell in (cell, x_cell):
            if dp is me and to_cell is cell:
                continue
            pl.semaphore_signal(
                barrier, inc=1, device_id=(dp, to_cell), device_id_type=pl.DeviceIdType.MESH
            )

    @pl.loop(1, half)
    def _(k):
        pl.semaphore_signal(
            barrier, inc=1, device_id=(me, (line + k) % half * 2 + x),
            device_id_type=pl.DeviceIdType.MESH,
        )

    square = (tile, tile)

    def column(row):
        return jnp.transpose(jnp.broadcast_to(row, square))

    v[...] = jnp.zeros_like(v)
    each("wait", small)
    root = jnp.sqrt(weights[...])
    tq[0] = root * residual[...]
    wcol = column(root)[:, 0:1]
    tcol[0] = column(tq[0])
    pl.semaphore_wait(barrier, 7 + half - 1)

    def half_of(ref, side):
        return ref.at[pl.ds(side * k_half, k_half)]

    def y_part(ref, p):
        return ref.at[pl.ds(core * k_half, k_half), :, pl.ds(p * LANES, LANES)]

    def y_copy(src, p, q):
        return remote(
            src, half_of(gy[p][q], core), y_s.at[p, q], y_r.at[p, q], y_peer, cell
        )

    def y_own(verb, p, q):
        pl.when(core == q)(lambda: each(verb, [y_copy(y_part(own_basis, p), p, q)]))

    def y_other(verb, p, q):
        pl.when(core != q)(lambda: each(verb, [y_copy(y_part(peer_basis, p), p, q)]))

    def swap(p, q, side):
        piece = half_of(gy[p][q], side)
        return remote(piece, piece, w_s.at[p, q], w_r.at[p, q], core_peer, cell)

    to_core = remote(own_basis, peer_basis, b_s.at[0], b_r.at[0], core_peer, cell)

    load_basis.wait()
    for q in range(2):
        y_own("start", order[0], q)
    to_core.start()

    t_targets = [
        (s, sources[(s // 4) * 2 + s % 2], x_cell if s // 2 % 2 else cell) for s in range(1, 8)
    ]
    t_copies = [
        remote(tq.at[0], tq.at[s], t_s.at[s], t_r.at[s], dp, to_cell)
        for s, dp, to_cell in t_targets
    ]
    each("start", t_copies)
    load_jac.wait()

    def lanes(n, dy=0, dc=0, sub=None):
        r, first, size = units[n]
        oy = 1 - y if dy else y
        oc = 1 - core if dc else core
        group = (oy * 2 + oc, oy * 2 + 1 - oc, (1 - oy) * 2, (1 - oy) * 2 + 1)[r]
        if sub is not None:
            first, size = first + sub[0], sub[1]
        return pl.ds(pl.multiple_of(group * width + first, LANES), size)

    def block_dot(n, b):
        r, first, size = units[n]
        held = (own_basis, peer_basis)[r] if r < 2 else gy[first // LANES][r - 2]
        if n == 0:
            for t in range(slot_count):
                at = slice(t * tile, (t + 1) * tile)
                keep = jnp.minimum(jnp.maximum(live[b] - t, 0), 1).astype(f32)
                jac[b, :, at] = jac[b, :, at] * keep.astype(jac.dtype)
        rows = [held[slots[b, t]] for t in range(slot_count)]
        return jnp.dot(jac[b], jnp.concatenate(rows, axis=0), preferred_element_type=f32)

    def part(refs, n, j):
        r, first, size = units[n]
        return [ref.at[r, j, :, first:first + size] for ref in refs]

    def x_copy(n, j):
        return pair(
            part((xq, xs), n, j), part((xrq, xrs), n, j), x_s, x_r, (n, j), (n, j), me, x_cell
        )

    def z_copy(n, j, slot):
        return pair(
            part((xrq, xrs), n, j), part((zrq, zrs), n, slot),
            z_s, z_r, (n, j), (n, slot), me, 2 * j + x,
        )

    def send_x(n):
        r, first, size = units[n]

        @pl.loop(0, half, unroll=4)
        def _(j):
            value, unit = code(block_dot(n, 2 * j + 1 - x))
            xq[r, j, :, first:first + size] = value
            xs[r, j, :, first:first + size] = unit
            each("start", x_copy(n, j))

    def send_z(n):
        r, first, size = units[n]
        cols = slice(first, first + size)

        def total(j):
            value = block_dot(n, 2 * j + x)
            each("wait_recv", x_copy(n, j))
            return value + decode(xrq[r, j, :, cols], xrs[r, j, :, cols])

        @pl.loop(1, half, unroll=3)
        def _(k):
            j = (line + k) % half
            value, unit = code(total(j))
            xrq[r, j, :, cols] = value
            xrs[r, j, :, cols] = unit
            each("start", z_copy(n, j, line))

        acc[r, :, cols] = total(line)

    def pass_on(p, q):
        y_copy(half_of(gy[p][q], core), p, q).wait_recv()
        swap(p, q, core).start()

    count = len(units)
    late = range(6, count)

    def part_held(slot, n, at_x):
        r, first, size = units[n]
        sub, condition = None, None
        if aligned:
            if slot in (2, 3) and r >= 2 and first != LANES:
                condition = first != 2 * LANES * (1 - at_x)
            if slot >= 4 and r < 2:
                sub = (at_x * LANES, 2 * LANES)
        return sub, condition

    def u_do(verb, n, slot):
        source, dp, to_cell = SOURCE.get(slot), core_peer, cell
        if slot == 2:
            dp, to_cell = me, x_cell
        elif slot == 4:
            dp = y_peer
        elif slot == 6 and n < 2:
            source, dp = 2, y_peer
        elif slot == 6 and n not in late:
            source, dp, to_cell = 4, me, x_cell
        elif slot == 6:
            source, dp, to_cell = 0, y_peer, x_cell
        if verb == "wait_recv":
            source = slot
        at_x = 1 - x if to_cell is x_cell and verb != "wait_recv" else x
        sub, condition = part_held(slot, n, at_x)
        cols = lanes(n, source // 4, source % 2, sub)

        def run():
            refs = [[ref.at[k, :, cols] for ref in (uq, us)] for k in (source, slot)]
            each(verb, pair(*refs, u_s, u_r, (slot, n), (slot, n), dp, to_cell))

        when(condition, run)

    place = {p: i * LANES for i, p in enumerate(order)}

    def turn(slot, first, size):
        cols = pl.ds(pl.multiple_of(first, LANES), size)
        value = decode(uq[slot, :, cols], us[slot, :, cols])
        term = value * tcol[slot][:, 0:1]
        v[:, cols] = v[:, cols] + jnp.sum(term.reshape(tile // 8, 8, size), axis=0)
        turned = jnp.transpose(value)
        high = turned.astype(jnp.bfloat16)
        at = slice(slot * tile, (slot + 1) * tile)
        ut[cols, at] = high
        at = slice((8 + slot) * tile, (9 + slot) * tile)
        ut[cols, at] = (turned - high.astype(f32)).astype(jnp.bfloat16)

    def own_columns(slot, p):
        cols = pl.ds(pl.multiple_of(me * width + p * LANES, LANES), LANES)
        value = decode(uq[slot, :, cols], us[slot, :, cols])
        high = value.astype(jnp.bfloat16)
        at = slice(place[p], place[p] + LANES)
        for k in (slot, 8 + slot):
            right[k * tile:(k + 1) * tile, at] = high
        right[(16 + slot) * tile:(17 + slot) * tile, at] = (
            value - high.astype(f32)
        ).astype(jnp.bfloat16)

    def take(n, slot):
        r, first, size = units[n]
        dy, dc = slot // 4, slot % 2
        oy, oc = (1 - y if dy else y), (1 - core if dc else core)
        start = (oy * 2 + oc, oy * 2 + 1 - oc, (1 - oy) * 2, (1 - oy) * 2 + 1)[r] * width + first
        if not aligned:
            turn(slot, start, size)
        elif r < 2:
            turn(slot, start + x * LANES, 2 * LANES)
        elif first == LANES:
            turn(slot, start, size)
        else:
            pl.when(first == 2 * LANES * x)(lambda: turn(slot, start, size))
        if r < 2 and not dy and r == dc:
            for p in order:
                own_columns(slot, p)
        if r >= 2 and dy:
            pl.when(core == r - 2)(lambda: own_columns(slot, first // LANES))

    def finish_rows(n):
        r, first, size = units[n]
        cols = slice(first, first + size)

        @pl.loop(1, half, unroll=3)
        def _(k):
            j = (line + k) % half
            each("wait_recv", z_copy(n, j, j))
            acc[r, :, cols] = acc[r, :, cols] + decode(
                zrq[r, j, :, cols], zrs[r, j, :, cols]
            )

        total = acc[r, :, cols]
        out = lanes(n)
        jq[:, out] = total
        scaled = total * wcol
        value, unit = code(scaled)
        uq[0, :, out] = value
        us[0, :, out] = unit
        for slot in (4, 6, 1) if n in late else (4, 1):
            u_do("start", n, slot)

    def arrived(n):
        swap(units[n][1] // LANES, units[n][0] - 2, 1 - core).wait_recv()

    def out_x(n):
        u_do("start", n, 2)

    def relay_y(n):
        u_do("wait_recv", n, 4)
        if 2 <= n and n not in late:
            u_do("start", n, 6)
        u_do("start", n, 5)

    def relay_x(n):
        u_do("wait_recv", n, 2)
        if n < 2:
            u_do("start", n, 6)
        u_do("start", n, 3)

    def relay_xy(n):
        u_do("wait_recv", n, 6)
        u_do("start", n, 7)

    def take_near(n):
        take(n, 0)
        u_do("wait_recv", n, 1)
        for slot in (1, 2, 4, 6):
            take(n, slot)

    def take_rest(n):
        for slot in (3, 5, 7):
            u_do("wait_recv", n, slot)
            take(n, slot)

    def to_rows(n):
        if n == 1:
            to_core.wait_recv()
            for q in range(2):
                y_other("start", order[0], q)
            for p in order[1:]:
                for q in range(2):
                    y_own("start", p, q)
                    y_other("start", p, q)
        if n >= 2:
            arrived(n)
        send_x(n)

    def on(n):
        p, q = units[n][1] // LANES, units[n][0] - 2
        if p != order[0]:
            pass_on(p, q)
            return
        for k in range(2):
            pl.when(core == k if q == 0 else core != k)(lambda: pass_on(p, k))

    def row_start(j):
        return (2 * j + x) * own_rows

    def window_start(j):
        return jnp.minimum(row_start(j) // LANES * LANES, full - window)

    def g_copy(i, j, slot):
        gq, gs, grq, grs = gbufs[i][1:]
        send, recv = g_sems[i]
        return pair(
            (gq.at[j], gs.at[j]), (grq.at[slot], grs.at[slot]), send, recv, (j,), (slot,),
            me, 2 * j + x,
        )

    def product(i):
        kind, first, size, rows = chunks[i]
        starts = [
            {"outer": j * width + 2 * x * LANES, "inner": j * width + LANES + x * rows,
             "all": row_start(j)}[kind] for j in range(half)
        ]

        def left(depth):
            return jnp.concatenate(
                [ut[pl.ds(pl.multiple_of(start, 16), rows), 0:depth] for start in starts], axis=0
            )

        at, deep = slice(first, first + size), 8 * tile
        value = jnp.dot(left(2 * deep), right[0:2 * deep, at], preferred_element_type=f32)
        value = value + jnp.dot(left(deep), right[2 * deep:, at], preferred_element_type=f32)
        gbufs[i][0][...] = value.reshape(half, rows, size)

    def own_place(i):
        kind, _, _, rows = chunks[i]
        if kind == "all":
            return pl.ds(0, rows)
        at = (x if kind == "outer" else 1 - x) * (own_rows - rows)
        return pl.ds(pl.multiple_of(at, 8), rows)

    def spans(i):
        _, first, size, _ = chunks[i]
        for p in order:
            if first <= place[p] < first + size:
                at = place[p] - first
                yield slice(p * LANES, (p + 1) * LANES), slice(at, at + LANES)

    def gram(i):
        product(i)

        @pl.loop(1, half, unroll=3)
        def _(k):
            j = (line + k) % half
            gq, gs = gbufs[i][1:3]
            value, unit = code(gbufs[i][0][j])
            gq[j] = value
            gs[j] = unit * (1.0 / ndata)
            each("start", g_copy(i, j, line))

    def s_pair(i, k):
        src, dst, dp = ((0, 1, core_peer), (0, 2, y_peer), (2, 3, core_peer))[k]
        sq, su = sbufs[i]
        send, recv = s_sems[i]
        return pair(
            (sq.at[src], su.at[src]), (sq.at[dst], su.at[dst]), send, recv, (k,), (k,), dp, cell
        )

    def s_sum(i):
        total = gbufs[i][0]
        grq, grs = gbufs[i][3:]
        total[line] = total[line] * (1.0 / ndata)

        @pl.loop(1, half, unroll=3)
        def _(k):
            j = (line + k) % half
            each("wait_recv", g_copy(i, j, j))
            total[line] = total[line] + decode(grq[j], grs[j])

        sq, su = sbufs[i]
        sq[0], su[0] = code(total[line])
        each("start", s_pair(i, 1))
        each("start", s_pair(i, 0))

    def s_relay(i):
        each("wait_recv", s_pair(i, 1))
        each("start", s_pair(i, 2))

    def s_finish(i, r):
        rows = chunks[i][3]
        sq, su = sbufs[i]
        at = own_place(i)
        row = lax.broadcasted_iota(jnp.int32, (rows, LANES), 0) + cell * own_rows + at.start
        col = lax.broadcasted_iota(jnp.int32, (rows, LANES), 1) + sources[r] * width
        for to, part in spans(i):
            value = decode(sq[r, :, part], su[r, :, part])
            out = pl.ds(pl.multiple_of(sources[r] * width + to.start, LANES), LANES)
            system[at, out] = value + (row == col + to.start).astype(f32)

    def vz_copy(j, slot):
        at = pl.ds(pl.multiple_of(window_start(j), LANES), window)
        return remote(v.at[:, at], vr.at[slot], vz_s.at[j], vz_r.at[slot], me, 2 * j + x)

    to_rows(0)
    to_rows(1)
    send_z(0)
    on(2)
    on(3)
    to_rows(3)
    send_z(1)
    on(4)
    to_rows(2)
    finish_rows(0)
    to_rows(4)
    send_z(3)
    on(5)
    to_rows(5)
    send_z(4)
    out_x(0)
    finish_rows(3)
    send_z(2)
    on(6)
    to_rows(6)
    send_z(5)
    finish_rows(4)
    finish_rows(1)
    out_x(1)
    finish_rows(2)
    relay_x(0)
    out_x(3)
    on(7)
    out_x(4)
    to_rows(7)
    send_z(6)
    finish_rows(5)
    relay_x(1)
    relay_y(3)
    relay_x(3)
    relay_y(4)
    relay_x(4)
    relay_y(0)
    out_x(2)
    relay_y(2)
    send_z(7)
    out_x(5)
    relay_y(1)
    relay_y(5)
    finish_rows(6)
    relay_xy(3)
    for s in range(1, 8):
        t_copies[s - 1].wait_recv()
        tcol[s] = column(tq[s])
    take_near(3)
    relay_xy(1)
    take_near(1)
    relay_xy(0)
    relay_xy(2)
    relay_xy(4)
    relay_x(2)
    take_near(0)
    take_near(2)
    out_x(6)
    relay_x(5)
    take_rest(1)
    relay_xy(5)
    take_near(4)
    take_near(5)
    finish_rows(7)
    take_rest(0)
    take_rest(3)
    take_rest(4)
    take_rest(2)
    out_x(7)
    take_rest(5)
    if aligned:
        gram(0)
    relay_y(7)
    relay_y(6)
    relay_x(6)
    relay_xy(6)
    relay_x(7)
    relay_xy(7)
    take_near(6)
    take_near(7)
    take_rest(6)
    take_rest(7)
    put_jq = pltpu.make_async_copy(jq, jq_out, in_s.at[6])
    put_jq.start()
    rest = range(1 if aligned else 0, len(chunks))
    for i in rest:
        gram(i)

    @pl.loop(1, half)
    def _(k):
        vz_copy((line + k) % half, line).start()

    if aligned:
        s_sum(0)
        s_finish(0, 0)
        s_relay(0)

    for i in rest:
        s_sum(i)

    vr[line] = v[:, pl.ds(pl.multiple_of(window_start(line), LANES), window)]
    total = vr[line]
    for k in range(1, half):
        j = (line + k) % half
        vz_copy(j, j).wait_recv()
        total = total + vr[j]
    misfit = jnp.sum(total, axis=0, keepdims=True) / math.sqrt(ndata)
    offset = row_start(line) - window_start(line)
    own = jnp.zeros(rhs.shape, f32)
    starts = [c * own_rows for c in range(n_cells)]
    for off in sorted({s - min(s // LANES * LANES, full - window) for s in starts}):
        own = jnp.where(offset == off, misfit[:, off:off + own_rows], own)
    rhs[...] = own

    put_rhs = pltpu.make_async_copy(rhs, rhs_out, in_s.at[7])
    put_rhs.start()
    if aligned:
        each("wait_recv", s_pair(0, 0))
        s_finish(0, 1)
        s_finish(0, 2)
        each("wait_recv", s_pair(0, 2))
        s_finish(0, 3)
    for i in rest:
        s_finish(i, 0)
        each("wait_recv", s_pair(i, 0))
        s_finish(i, 1)
    for i in rest:
        s_relay(i)
        s_finish(i, 2)
    for i in rest:
        each("wait_recv", s_pair(i, 2))
        s_finish(i, 3)

    put_system = pltpu.make_async_copy(system, system_out, in_s.at[8])
    put_system.start()
    to_core.wait_send()
    for p in order:
        for q in range(2):
            y_own("wait_send", p, q)
            y_other("wait_send", p, q)
            swap(p, q, core).wait_send()
    for n in range(count):
        for slot in range(1, 8):
            u_do("wait_send", n, slot)
    each("wait_send", t_copies)
    for i in range(len(chunks)):
        for k in range(3):
            each("wait_send", s_pair(i, k))

    @pl.loop(0, half)
    def _(j):
        for n in range(count):
            each("wait_send", x_copy(n, j))

    @pl.loop(1, half)
    def _(k):
        j = (line + k) % half
        for n in range(count):
            each("wait_send", z_copy(n, j, line))
        for i in range(len(chunks)):
            each("wait_send", g_copy(i, j, line))
        vz_copy(j, line).wait_send()

    put_jq.wait()
    put_rhs.wait()
    put_system.wait()


def hand_over(parts, *refs):
    count = len(refs) // 3
    sems = refs[-1]
    steps = []
    for i in range(count):
        source, to, held = refs[i], refs[count + i], refs[2 * count + i]
        rows = source.shape[0] // parts[i]
        for k in range(parts[i]):
            at = pl.ds(k * rows, rows)
            n = len(steps)
            steps.append((
                pltpu.make_async_copy(source.at[at], held.at[at], sems.at[0, n]),
                pltpu.make_async_copy(held.at[at], to.at[at], sems.at[1, n]),
            ))
    for read, _ in steps:
        read.start()
    for read, write in steps:
        read.wait()
        write.start()
    for _, write in steps:
        write.wait()


def on_device(jac_blocks, slot_cell_blocks, live_counts, eigen_basis, weights, residual):
    n_cells = lax.axis_size("cells")
    n_groups = lax.axis_size("dp")
    half = n_cells // 2
    tile = jac_blocks.shape[1]
    depth, width = eigen_basis.shape
    full = width * n_groups
    rows_here = full // n_cells
    ndata = weights.shape[0] * n_cells * n_groups
    pieces = width // LANES
    assert n_groups == 4 and n_cells % 2 == 0 and pieces == 3
    assert jac_blocks.shape[0] == n_cells and weights.shape[0] == tile
    aligned = 2 * rows_here == width
    order = (0, 2, 1)
    units = [(0, 0, width), (1, 0, width)]
    for p in order:
        units += [(2, p * LANES, LANES), (3, p * LANES, LANES)]
    window = 2 * LANES
    if aligned:
        chunks = (
            ("outer", 0, 2 * LANES, LANES),
            ("outer", 2 * LANES, LANES, LANES),
            ("inner", 0, width, rows_here - LANES),
        )
    else:
        chunks = (("all", 0, width, rows_here),)
    f32, bf16, i16 = jnp.float32, jnp.bfloat16, jnp.int16
    anywhere = pl.BlockSpec(memory_space=pl.ANY)

    def sems(*shape):
        return [pltpu.SemaphoreType.DMA(shape)] * 2

    def coded(*lead, rows, columns):
        return [pltpu.VMEM((*lead, rows, columns), i16), pltpu.VMEM((*lead, 1, columns), f32)]

    gbufs = tuple(
        (pltpu.VMEM((half, rows, size), f32), *(coded(half, rows=rows, columns=size) * 2))
        for _, _, size, rows in chunks
    )
    blocks = depth // tile
    jq, system, rhs = pl.pallas_call(
        functools.partial(fused, n_cells, ndata, tuple(units), order, chunks, aligned),
        out_shape=(
            jax.ShapeDtypeStruct((tile, full), f32),
            jax.ShapeDtypeStruct((rows_here, full), f32),
            jax.ShapeDtypeStruct((1, rows_here), f32),
        ),
        in_specs=[anywhere] * 6,
        out_specs=(anywhere,) * 3,
        scratch_shapes=[
            pltpu.SMEM(slot_cell_blocks.shape, jnp.int32),
            pltpu.SMEM((live_counts.shape[0],), jnp.int32),
            pltpu.VMEM((1, tile), f32),
            pltpu.VMEM((1, tile), f32),
            pltpu.VMEM((tile, full), f32),
            pltpu.VMEM((rows_here, full), f32),
            pltpu.VMEM((1, rows_here), f32),
            pltpu.VMEM((blocks, tile, width), bf16),
            pltpu.VMEM((blocks, tile, width), bf16),
            ((pltpu.VMEM((blocks, tile, LANES), bf16),) * 2,) * pieces,
            pltpu.VMEM(jac_blocks.shape, bf16),
            *coded(4, half, rows=tile, columns=width),
            *coded(4, half, rows=tile, columns=width),
            *coded(4, half, rows=tile, columns=width),
            pltpu.VMEM((4, tile, width), f32),
            *coded(8, rows=tile, columns=full),
            pltpu.VMEM((full, 16 * tile), bf16),
            pltpu.VMEM((24 * tile, width), bf16),
            pltpu.VMEM((8, full), f32),
            pltpu.VMEM((8, 1, tile), f32),
            pltpu.VMEM((8, tile, tile), f32),
            gbufs,
            tuple(tuple(coded(4, rows=c[3], columns=c[2])) for c in chunks),
            pltpu.VMEM((half, 8, window), f32),
            pltpu.SemaphoreType.DMA((9,)),
            *sems(1), *sems(pieces, 2), *sems(pieces, 2),
            *sems(2, len(units), half), *sems(2, len(units), half),
            *sems(2, 8, len(units)), *sems(8), *sems(half),
            tuple(tuple(sems(2, half)) for _ in chunks),
            tuple(tuple(sems(2, 3)) for _ in chunks),
        ],
        compiler_params=pltpu.CompilerParams(
            collective_id=0, has_side_effects=True, vmem_limit_bytes=60 * 1024 * 1024
        ),
    )(
        slot_cell_blocks, live_counts[:, 0], jac_blocks,
        eigen_basis.reshape(blocks, tile, width), weights[None], residual[None],
    )
    done = (jq, system, rhs)
    parts = tuple(next(k for k in (4, 2, 1) if k == 1 or a.shape[0] % (8 * k) == 0) for a in done)
    jq, system, rhs = pl.pallas_call(
        functools.partial(hand_over, parts),
        out_shape=tuple(jax.ShapeDtypeStruct(a.shape, a.dtype) for a in done),
        in_specs=[anywhere] * 3,
        out_specs=(anywhere,) * 3,
        scratch_shapes=[
            *(pltpu.VMEM(a.shape, a.dtype) for a in done),
            pltpu.SemaphoreType.DMA((2, sum(parts))),
        ],
    )(*done)
    return jq, system, rhs[0]


def solution(mesh):
    placed = (
        P("dp", None, "cells"),
        P("dp", "cells"),
        P("dp", "cells"),
        P("cells", "dp"),
        P(("dp", "cells")),
        P(("dp", "cells")),
    )
    return jax.shard_map(
        on_device,
        mesh=mesh,
        in_specs=placed,
        out_specs=(P(("dp", "cells"), None), P("cells", None), P("cells")),
        check_vma=False,
    )
```

```python
import functools
import math

import jax
import jax.numpy as jnp
from jax import lax
from jax.experimental import pallas as pl
from jax.experimental.pallas import tpu as pltpu
from jax.sharding import PartitionSpec as P

LANES = 128
SOURCE = {1: 0, 2: 0, 4: 0, 3: 2, 5: 4, 7: 6}


def code(value):
    top = jnp.maximum(jnp.max(jnp.abs(value), axis=0, keepdims=True), 1e-30)
    whole = jnp.round(value * (32767.0 / top))
    return whole.astype(jnp.int32).astype(jnp.int16), top * (1.0 / 32767.0)


def decode(whole, unit):
    return whole.astype(jnp.int32).astype(jnp.float32) * unit


def fused(
    n_cells, ndata, units, order, chunks, aligned,
    slots_in, live_in, jac_in, basis_in, weights_in, residual_in,
    jq_out, system_out, rhs_out,
    slots, live, weights, residual, jq, system, rhs,
    own_basis, peer_basis, gy, jac, xq, xs, xrq, xrs, zrq, zrs, acc, uq, us, ut, right, v,
    tq, tcol, gbufs, sbufs, vr,
    in_s, b_s, b_r, y_s, y_r, w_s, w_r, x_s, x_r, z_s, z_r, u_s, u_r, t_s, t_r,
    vz_s, vz_r, g_sems, s_sems,
):
    f32 = jnp.float32
    half = n_cells // 2
    tile = jac.shape[1]
    slot_count = jac.shape[2] // tile
    width = basis_in.shape[2]
    full = uq.shape[2]
    own_rows = system.shape[0]
    k_half = own_basis.shape[0] // 2
    window = vr.shape[2]
    me, cell = lax.axis_index("dp"), lax.axis_index("cells")
    core, y = me % 2, me // 2
    core_peer = y * 2 + 1 - core
    y_peer = (1 - y) * 2 + core
    far_peer = (1 - y) * 2 + 1 - core
    sources = (me, core_peer, y_peer, far_peer)
    x, line = cell % 2, cell // 2
    x_cell = line * 2 + 1 - x

    def remote(src, dst, send, recv, dp, to_cell):
        return pltpu.make_async_remote_copy(
            src_ref=src, dst_ref=dst, send_sem=send, recv_sem=recv,
            device_id=(dp, to_cell), device_id_type=pl.DeviceIdType.MESH,
        )

    def pair(src, dst, send, recv, at, to, dp, to_cell):
        return [
            remote(src[i], dst[i], send.at[(i, *at)], recv.at[(i, *to)], dp, to_cell)
            for i in range(2)
        ]

    def each(verb, copies):
        for copy in copies:
            getattr(copy, verb)()

    def when(condition, run):
        if condition is None:
            run()
        else:
            pl.when(condition)(run)

    load_basis = pltpu.make_async_copy(basis_in, own_basis, in_s.at[0])
    load_jac = pltpu.make_async_copy(jac_in, jac, in_s.at[1])
    load_basis.start()
    small = [
        pltpu.make_async_copy(src, dst, in_s.at[2 + i])
        for i, (src, dst) in enumerate((
            (weights_in, weights), (residual_in, residual), (slots_in, slots), (live_in, live)
        ))
    ]
    each("start", small)
    load_jac.start()

    barrier = pltpu.get_barrier_semaphore()
    for dp in sources:
        for to_cell in (cell, x_cell):
            if dp is me and to_cell is cell:
                continue
            pl.semaphore_signal(
                barrier, inc=1, device_id=(dp, to_cell), device_id_type=pl.DeviceIdType.MESH
            )

    @pl.loop(1, half)
    def _(k):
        pl.semaphore_signal(
            barrier, inc=1, device_id=(me, (line + k) % half * 2 + x),
            device_id_type=pl.DeviceIdType.MESH,
        )

    pl.semaphore_wait(barrier, 7 + half - 1)

    def half_of(ref, side):
        return ref.at[pl.ds(side * k_half, k_half)]

    def y_part(ref, p):
        return ref.at[pl.ds(core * k_half, k_half), :, pl.ds(p * LANES, LANES)]

    def y_copy(src, p, q):
        return remote(
            src, half_of(gy[p][q], core), y_s.at[p, q], y_r.at[p, q], y_peer, cell
        )

    def y_own(verb, p, q):
        pl.when(core == q)(lambda: each(verb, [y_copy(y_part(own_basis, p), p, q)]))

    def y_other(verb, p, q):
        pl.when(core != q)(lambda: each(verb, [y_copy(y_part(peer_basis, p), p, q)]))

    def swap(p, q, side):
        piece = half_of(gy[p][q], side)
        return remote(piece, piece, w_s.at[p, q], w_r.at[p, q], core_peer, cell)

    to_core = remote(own_basis, peer_basis, b_s.at[0], b_r.at[0], core_peer, cell)

    load_basis.wait()
    for q in range(2):
        y_own("start", order[0], q)
    to_core.start()

    square = (tile, tile)

    def column(row):
        return jnp.transpose(jnp.broadcast_to(row, square))

    v[...] = jnp.zeros_like(v)
    each("wait", small)
    root = jnp.sqrt(weights[...])
    tq[0] = root * residual[...]
    wcol = column(root)[:, 0:1]
    tcol[0] = column(tq[0])

    t_targets = [
        (s, sources[(s // 4) * 2 + s % 2], x_cell if s // 2 % 2 else cell) for s in range(1, 8)
    ]
    t_copies = [
        remote(tq.at[0], tq.at[s], t_s.at[s], t_r.at[s], dp, to_cell)
        for s, dp, to_cell in t_targets
    ]
    each("start", t_copies)
    load_jac.wait()

    def lanes(n, dy=0, dc=0, sub=None):
        r, first, size = units[n]
        oy = 1 - y if dy else y
        oc = 1 - core if dc else core
        group = (oy * 2 + oc, oy * 2 + 1 - oc, (1 - oy) * 2, (1 - oy) * 2 + 1)[r]
        if sub is not None:
            first, size = first + sub[0], sub[1]
        return pl.ds(pl.multiple_of(group * width + first, LANES), size)

    def block_dot(n, b):
        r, first, size = units[n]
        held = (own_basis, peer_basis)[r] if r < 2 else gy[first // LANES][r - 2]
        if n == 0:
            for t in range(slot_count):
                at = slice(t * tile, (t + 1) * tile)
                keep = jnp.minimum(jnp.maximum(live[b] - t, 0), 1).astype(f32)
                jac[b, :, at] = jac[b, :, at] * keep.astype(jac.dtype)
        rows = [held[slots[b, t]] for t in range(slot_count)]
        return jnp.dot(jac[b], jnp.concatenate(rows, axis=0), preferred_element_type=f32)

    def part(refs, n, j):
        r, first, size = units[n]
        return [ref.at[r, j, :, first:first + size] for ref in refs]

    def x_copy(n, j):
        return pair(
            part((xq, xs), n, j), part((xrq, xrs), n, j), x_s, x_r, (n, j), (n, j), me, x_cell
        )

    def z_copy(n, j, slot):
        return pair(
            part((xrq, xrs), n, j), part((zrq, zrs), n, slot),
            z_s, z_r, (n, j), (n, slot), me, 2 * j + x,
        )

    def send_x(n):
        r, first, size = units[n]

        @pl.loop(0, half, unroll=1)
        def _(j):
            value, unit = code(block_dot(n, 2 * j + 1 - x))
            xq[r, j, :, first:first + size] = value
            xs[r, j, :, first:first + size] = unit
            each("start", x_copy(n, j))

    def send_z(n):
        r, first, size = units[n]
        cols = slice(first, first + size)

        def total(j):
            value = block_dot(n, 2 * j + x)
            each("wait_recv", x_copy(n, j))
            return value + decode(xrq[r, j, :, cols], xrs[r, j, :, cols])

        @pl.loop(1, half, unroll=1)
        def _(k):
            j = (line + k) % half
            value, unit = code(total(j))
            xrq[r, j, :, cols] = value
            xrs[r, j, :, cols] = unit
            each("start", z_copy(n, j, line))

        acc[r, :, cols] = total(line)

    def pass_on(p, q):
        y_copy(half_of(gy[p][q], core), p, q).wait_recv()
        swap(p, q, core).start()

    count = len(units)
    late = range(6, count)

    def part_held(slot, n, at_x):
        r, first, size = units[n]
        sub, condition = None, None
        if aligned:
            if slot in (2, 3) and r >= 2 and first != LANES:
                condition = first != 2 * LANES * (1 - at_x)
            if slot >= 4 and r < 2:
                sub = (at_x * LANES, 2 * LANES)
        return sub, condition

    def u_do(verb, n, slot):
        source, dp, to_cell = SOURCE.get(slot), core_peer, cell
        if slot == 2:
            dp, to_cell = me, x_cell
        elif slot == 4:
            dp = y_peer
        elif slot == 6 and n < 2:
            source, dp = 2, y_peer
        elif slot == 6 and n not in late:
            source, dp, to_cell = 4, me, x_cell
        elif slot == 6:
            source, dp, to_cell = 0, y_peer, x_cell
        if verb == "wait_recv":
            source = slot
        at_x = 1 - x if to_cell is x_cell and verb != "wait_recv" else x
        sub, condition = part_held(slot, n, at_x)
        cols = lanes(n, source // 4, source % 2, sub)

        def run():
            refs = [[ref.at[k, :, cols] for ref in (uq, us)] for k in (source, slot)]
            each(verb, pair(*refs, u_s, u_r, (slot, n), (slot, n), dp, to_cell))

        when(condition, run)

    place = {p: i * LANES for i, p in enumerate(order)}

    def turn(slot, first, size):
        cols = pl.ds(pl.multiple_of(first, LANES), size)
        value = decode(uq[slot, :, cols], us[slot, :, cols])
        term = value * tcol[slot][:, 0:1]
        v[:, cols] = v[:, cols] + jnp.sum(term.reshape(tile // 8, 8, size), axis=0)
        turned = jnp.transpose(value)
        high = turned.astype(jnp.bfloat16)
        at = slice(slot * tile, (slot + 1) * tile)
        ut[cols, at] = high
        at = slice((8 + slot) * tile, (9 + slot) * tile)
        ut[cols, at] = (turned - high.astype(f32)).astype(jnp.bfloat16)

    def own_columns(slot, p):
        cols = pl.ds(pl.multiple_of(me * width + p * LANES, LANES), LANES)
        value = decode(uq[slot, :, cols], us[slot, :, cols])
        high = value.astype(jnp.bfloat16)
        at = slice(place[p], place[p] + LANES)
        for k in (slot, 8 + slot):
            right[k * tile:(k + 1) * tile, at] = high
        right[(16 + slot) * tile:(17 + slot) * tile, at] = (
            value - high.astype(f32)
        ).astype(jnp.bfloat16)

    def take(n, slot):
        r, first, size = units[n]
        dy, dc = slot // 4, slot % 2
        oy, oc = (1 - y if dy else y), (1 - core if dc else core)
        start = (oy * 2 + oc, oy * 2 + 1 - oc, (1 - oy) * 2, (1 - oy) * 2 + 1)[r] * width + first
        if not aligned:
            turn(slot, start, size)
        elif r < 2:
            turn(slot, start + x * LANES, 2 * LANES)
        elif first == LANES:
            turn(slot, start, size)
        else:
            pl.when(first == 2 * LANES * x)(lambda: turn(slot, start, size))
        if r < 2 and not dy and r == dc:
            for p in order:
                own_columns(slot, p)
        if r >= 2 and dy:
            pl.when(core == r - 2)(lambda: own_columns(slot, first // LANES))

    def finish_rows(n):
        r, first, size = units[n]
        cols = slice(first, first + size)

        @pl.loop(1, half, unroll=3)
        def _(k):
            j = (line + k) % half
            each("wait_recv", z_copy(n, j, j))
            acc[r, :, cols] = acc[r, :, cols] + decode(
                zrq[r, j, :, cols], zrs[r, j, :, cols]
            )

        total = acc[r, :, cols]
        out = lanes(n)
        jq[:, out] = total
        scaled = total * wcol
        value, unit = code(scaled)
        uq[0, :, out] = value
        us[0, :, out] = unit
        for slot in (4, 6, 1) if n in late else (4, 1):
            u_do("start", n, slot)

    def arrived(n):
        swap(units[n][1] // LANES, units[n][0] - 2, 1 - core).wait_recv()

    def out_x(n):
        u_do("start", n, 2)

    def relay_y(n):
        u_do("wait_recv", n, 4)
        if 2 <= n and n not in late:
            u_do("start", n, 6)
        u_do("start", n, 5)

    def relay_x(n):
        u_do("wait_recv", n, 2)
        if n < 2:
            u_do("start", n, 6)
        u_do("start", n, 3)

    def relay_xy(n):
        u_do("wait_recv", n, 6)
        u_do("start", n, 7)

    def take_near(n):
        take(n, 0)
        u_do("wait_recv", n, 1)
        for slot in (1, 2, 4, 6):
            take(n, slot)

    def take_rest(n):
        for slot in (3, 5, 7):
            u_do("wait_recv", n, slot)
            take(n, slot)

    def to_rows(n):
        if n == 1:
            to_core.wait_recv()
            for q in range(2):
                y_other("start", order[0], q)
            for p in order[1:]:
                for q in range(2):
                    y_own("start", p, q)
                    y_other("start", p, q)
        if n >= 2:
            arrived(n)
        send_x(n)

    def on(n):
        p, q = units[n][1] // LANES, units[n][0] - 2
        if p != order[0]:
            pass_on(p, q)
            return
        for k in range(2):
            pl.when(core == k if q == 0 else core != k)(lambda: pass_on(p, k))

    def row_start(j):
        return (2 * j + x) * own_rows

    def window_start(j):
        return jnp.minimum(row_start(j) // LANES * LANES, full - window)

    def g_copy(i, j, slot):
        gq, gs, grq, grs = gbufs[i][1:]
        send, recv = g_sems[i]
        return pair(
            (gq.at[j], gs.at[j]), (grq.at[slot], grs.at[slot]), send, recv, (j,), (slot,),
            me, 2 * j + x,
        )

    def first_row(i, j):
        kind, _, _, rows = chunks[i]
        start = {"outer": j * width + 2 * x * LANES, "inner": j * width + LANES + x * rows,
                 "all": row_start(j)}[kind]
        return pl.ds(pl.multiple_of(start, 16), rows)

    def times_right(i, left):
        _, first, size, _ = chunks[i]
        at, deep = slice(first, first + size), 8 * tile
        value = jnp.dot(left(2 * deep), right[0:2 * deep, at], preferred_element_type=f32)
        return value + jnp.dot(left(deep), right[2 * deep:, at], preferred_element_type=f32)

    def product(i):
        _, _, size, rows = chunks[i]
        value = times_right(i, lambda depth: jnp.concatenate(
            [ut[first_row(i, j), 0:depth] for j in range(half)], axis=0
        ))
        gbufs[i][0][...] = value.reshape(half, rows, size)

    def line_product(i, j):
        gbufs[i][0][j] = times_right(i, lambda depth: ut[first_row(i, j), 0:depth])

    def own_place(i):
        kind, _, _, rows = chunks[i]
        if kind == "all":
            return pl.ds(0, rows)
        at = (x if kind == "outer" else 1 - x) * (own_rows - rows)
        return pl.ds(pl.multiple_of(at, 8), rows)

    def spans(i):
        _, first, size, _ = chunks[i]
        for p in order:
            if first <= place[p] < first + size:
                at = place[p] - first
                yield slice(p * LANES, (p + 1) * LANES), slice(at, at + LANES)

    def gram(i, by_line=False):
        if not by_line:
            product(i)

        @pl.loop(1, half, unroll=1 if by_line else 3)
        def _(k):
            j = (line + k) % half
            if by_line:
                line_product(i, j)
            gq, gs = gbufs[i][1:3]
            value, unit = code(gbufs[i][0][j])
            gq[j] = value
            gs[j] = unit * (1.0 / ndata)
            each("start", g_copy(i, j, line))

    def s_pair(i, k):
        src, dst, dp = ((0, 1, core_peer), (0, 2, y_peer), (2, 3, core_peer))[k]
        sq, su = sbufs[i]
        send, recv = s_sems[i]
        return pair(
            (sq.at[src], su.at[src]), (sq.at[dst], su.at[dst]), send, recv, (k,), (k,), dp, cell
        )

    def s_sum(i):
        total = gbufs[i][0]
        grq, grs = gbufs[i][3:]
        total[line] = total[line] * (1.0 / ndata)

        @pl.loop(1, half, unroll=3)
        def _(k):
            j = (line + k) % half
            each("wait_recv", g_copy(i, j, j))
            total[line] = total[line] + decode(grq[j], grs[j])

        sq, su = sbufs[i]
        sq[0], su[0] = code(total[line])
        each("start", s_pair(i, 1))
        each("start", s_pair(i, 0))

    def s_relay(i):
        each("wait_recv", s_pair(i, 1))
        each("start", s_pair(i, 2))

    def s_finish(i, r):
        rows = chunks[i][3]
        sq, su = sbufs[i]
        at = own_place(i)
        row = lax.broadcasted_iota(jnp.int32, (rows, LANES), 0) + cell * own_rows + at.start
        col = lax.broadcasted_iota(jnp.int32, (rows, LANES), 1) + sources[r] * width
        for to, part in spans(i):
            value = decode(sq[r, :, part], su[r, :, part])
            out = pl.ds(pl.multiple_of(sources[r] * width + to.start, LANES), LANES)
            system[at, out] = value + (row == col + to.start).astype(f32)

    def vz_copy(j, slot):
        at = pl.ds(pl.multiple_of(window_start(j), LANES), window)
        return remote(v.at[:, at], vr.at[slot], vz_s.at[j], vz_r.at[slot], me, 2 * j + x)

    to_rows(0)
    to_rows(1)
    send_z(0)
    on(2)
    on(3)
    to_rows(3)
    send_z(1)
    on(4)
    to_rows(2)
    finish_rows(0)
    to_rows(4)
    send_z(3)
    on(5)
    to_rows(5)
    send_z(4)
    out_x(0)
    finish_rows(3)
    send_z(2)
    on(6)
    to_rows(6)
    send_z(5)
    finish_rows(4)
    finish_rows(1)
    out_x(1)
    finish_rows(2)
    relay_x(0)
    out_x(3)
    on(7)
    out_x(4)
    to_rows(7)
    send_z(6)
    finish_rows(5)
    relay_x(1)
    relay_y(3)
    relay_x(3)
    relay_y(4)
    relay_x(4)
    relay_y(0)
    out_x(2)
    relay_y(2)
    send_z(7)
    out_x(5)
    relay_y(1)
    relay_y(5)
    finish_rows(6)
    relay_xy(3)
    for s in range(1, 8):
        t_copies[s - 1].wait_recv()
        tcol[s] = column(tq[s])
    take_near(3)
    relay_xy(1)
    take_near(1)
    relay_xy(0)
    relay_xy(2)
    relay_xy(4)
    relay_x(2)
    take_near(0)
    take_near(2)
    out_x(6)
    relay_x(5)
    take_rest(1)
    relay_xy(5)
    take_near(4)
    take_near(5)
    finish_rows(7)
    take_rest(0)
    take_rest(3)
    take_rest(4)
    take_rest(2)
    out_x(7)
    take_rest(5)
    if aligned:
        gram(0, by_line=True)
    relay_y(7)
    relay_y(6)
    relay_x(6)
    relay_xy(6)
    relay_x(7)
    relay_xy(7)
    take_near(6)
    take_near(7)
    take_rest(6)
    take_rest(7)
    put_jq = pltpu.make_async_copy(jq, jq_out, in_s.at[6])
    put_jq.start()
    rest = range(1 if aligned else 0, len(chunks))
    for i in rest:
        gram(i)

    @pl.loop(1, half)
    def _(k):
        vz_copy((line + k) % half, line).start()

    if aligned:
        line_product(0, line)
        s_sum(0)
        s_finish(0, 0)
        s_relay(0)

    for i in rest:
        s_sum(i)

    vr[line] = v[:, pl.ds(pl.multiple_of(window_start(line), LANES), window)]
    total = vr[line]
    for k in range(1, half):
        j = (line + k) % half
        vz_copy(j, j).wait_recv()
        total = total + vr[j]
    misfit = jnp.sum(total, axis=0, keepdims=True) / math.sqrt(ndata)
    offset = row_start(line) - window_start(line)
    own = jnp.zeros(rhs.shape, f32)
    starts = [c * own_rows for c in range(n_cells)]
    for off in sorted({s - min(s // LANES * LANES, full - window) for s in starts}):
        own = jnp.where(offset == off, misfit[:, off:off + own_rows], own)
    rhs[...] = own

    put_rhs = pltpu.make_async_copy(rhs, rhs_out, in_s.at[7])
    put_rhs.start()
    if aligned:
        each("wait_recv", s_pair(0, 0))
        s_finish(0, 1)
        s_finish(0, 2)
        each("wait_recv", s_pair(0, 2))
        s_finish(0, 3)
    for i in rest:
        s_finish(i, 0)
        each("wait_recv", s_pair(i, 0))
        s_finish(i, 1)
    for i in rest:
        s_relay(i)
        s_finish(i, 2)
    for i in rest:
        each("wait_recv", s_pair(i, 2))
        s_finish(i, 3)

    put_system = pltpu.make_async_copy(system, system_out, in_s.at[8])
    put_system.start()
    to_core.wait_send()
    for p in order:
        for q in range(2):
            y_own("wait_send", p, q)
            y_other("wait_send", p, q)
            swap(p, q, core).wait_send()
    for n in range(count):
        for slot in range(1, 8):
            u_do("wait_send", n, slot)
    each("wait_send", t_copies)
    for i in range(len(chunks)):
        for k in range(3):
            each("wait_send", s_pair(i, k))

    @pl.loop(0, half)
    def _(j):
        for n in range(count):
            each("wait_send", x_copy(n, j))

    @pl.loop(1, half)
    def _(k):
        j = (line + k) % half
        for n in range(count):
            each("wait_send", z_copy(n, j, line))
        for i in range(len(chunks)):
            each("wait_send", g_copy(i, j, line))
        vz_copy(j, line).wait_send()

    put_jq.wait()
    put_rhs.wait()
    put_system.wait()


def hand_over(parts, *refs):
    count = len(refs) // 3
    sems = refs[-1]
    steps = []
    for i in range(count):
        source, to, held = refs[i], refs[count + i], refs[2 * count + i]
        rows = source.shape[0] // parts[i]
        for k in range(parts[i]):
            at = pl.ds(k * rows, rows)
            n = len(steps)
            steps.append((
                pltpu.make_async_copy(source.at[at], held.at[at], sems.at[0, n]),
                pltpu.make_async_copy(held.at[at], to.at[at], sems.at[1, n]),
            ))
    for read, _ in steps:
        read.start()
    for read, write in steps:
        read.wait()
        write.start()
    for _, write in steps:
        write.wait()


def on_device(jac_blocks, slot_cell_blocks, live_counts, eigen_basis, weights, residual):
    n_cells = lax.axis_size("cells")
    n_groups = lax.axis_size("dp")
    half = n_cells // 2
    tile = jac_blocks.shape[1]
    depth, width = eigen_basis.shape
    full = width * n_groups
    rows_here = full // n_cells
    ndata = weights.shape[0] * n_cells * n_groups
    pieces = width // LANES
    assert n_groups == 4 and n_cells % 2 == 0 and pieces == 3
    assert jac_blocks.shape[0] == n_cells and weights.shape[0] == tile
    aligned = 2 * rows_here == width
    order = (0, 2, 1)
    units = [(0, 0, width), (1, 0, width)]
    for p in order:
        units += [(2, p * LANES, LANES), (3, p * LANES, LANES)]
    window = 2 * LANES
    if aligned:
        chunks = (
            ("outer", 0, 2 * LANES, LANES),
            ("outer", 2 * LANES, LANES, LANES),
            ("inner", 0, width, rows_here - LANES),
        )
    else:
        chunks = (("all", 0, width, rows_here),)
    f32, bf16, i16 = jnp.float32, jnp.bfloat16, jnp.int16
    anywhere = pl.BlockSpec(memory_space=pl.ANY)

    def sems(*shape):
        return [pltpu.SemaphoreType.DMA(shape)] * 2

    def coded(*lead, rows, columns):
        return [pltpu.VMEM((*lead, rows, columns), i16), pltpu.VMEM((*lead, 1, columns), f32)]

    gbufs = tuple(
        (pltpu.VMEM((half, rows, size), f32), *(coded(half, rows=rows, columns=size) * 2))
        for _, _, size, rows in chunks
    )
    blocks = depth // tile
    jq, system, rhs = pl.pallas_call(
        functools.partial(fused, n_cells, ndata, tuple(units), order, chunks, aligned),
        out_shape=(
            jax.ShapeDtypeStruct((tile, full), f32),
            jax.ShapeDtypeStruct((rows_here, full), f32),
            jax.ShapeDtypeStruct((1, rows_here), f32),
        ),
        in_specs=[anywhere] * 6,
        out_specs=(anywhere,) * 3,
        scratch_shapes=[
            pltpu.SMEM(slot_cell_blocks.shape, jnp.int32),
            pltpu.SMEM((live_counts.shape[0],), jnp.int32),
            pltpu.VMEM((1, tile), f32),
            pltpu.VMEM((1, tile), f32),
            pltpu.VMEM((tile, full), f32),
            pltpu.VMEM((rows_here, full), f32),
            pltpu.VMEM((1, rows_here), f32),
            pltpu.VMEM((blocks, tile, width), bf16),
            pltpu.VMEM((blocks, tile, width), bf16),
            ((pltpu.VMEM((blocks, tile, LANES), bf16),) * 2,) * pieces,
            pltpu.VMEM(jac_blocks.shape, bf16),
            *coded(4, half, rows=tile, columns=width),
            *coded(4, half, rows=tile, columns=width),
            *coded(4, half, rows=tile, columns=width),
            pltpu.VMEM((4, tile, width), f32),
            *coded(8, rows=tile, columns=full),
            pltpu.VMEM((full, 16 * tile), bf16),
            pltpu.VMEM((24 * tile, width), bf16),
            pltpu.VMEM((8, full), f32),
            pltpu.VMEM((8, 1, tile), f32),
            pltpu.VMEM((8, tile, tile), f32),
            gbufs,
            tuple(tuple(coded(4, rows=c[3], columns=c[2])) for c in chunks),
            pltpu.VMEM((half, 8, window), f32),
            pltpu.SemaphoreType.DMA((9,)),
            *sems(1), *sems(pieces, 2), *sems(pieces, 2),
            *sems(2, len(units), half), *sems(2, len(units), half),
            *sems(2, 8, len(units)), *sems(8), *sems(half),
            tuple(tuple(sems(2, half)) for _ in chunks),
            tuple(tuple(sems(2, 3)) for _ in chunks),
        ],
        compiler_params=pltpu.CompilerParams(
            collective_id=0, has_side_effects=True, vmem_limit_bytes=60 * 1024 * 1024
        ),
    )(
        slot_cell_blocks, live_counts[:, 0], jac_blocks,
        eigen_basis.reshape(blocks, tile, width), weights[None], residual[None],
    )
    done = (jq, system, rhs)
    parts = tuple(next(k for k in (4, 2, 1) if k == 1 or a.shape[0] % (8 * k) == 0) for a in done)
    jq, system, rhs = pl.pallas_call(
        functools.partial(hand_over, parts),
        out_shape=tuple(jax.ShapeDtypeStruct(a.shape, a.dtype) for a in done),
        in_specs=[anywhere] * 3,
        out_specs=(anywhere,) * 3,
        scratch_shapes=[
            *(pltpu.VMEM(a.shape, a.dtype) for a in done),
            pltpu.SemaphoreType.DMA((2, sum(parts))),
        ],
    )(*done)
    return jq, system, rhs[0]


def solution(mesh):
    placed = (
        P("dp", None, "cells"),
        P("dp", "cells"),
        P("dp", "cells"),
        P("cells", "dp"),
        P(("dp", "cells")),
        P(("dp", "cells")),
    )
    return jax.shard_map(
        on_device,
        mesh=mesh,
        in_specs=placed,
        out_specs=(P(("dp", "cells"), None), P("cells", None), P("cells")),
        check_vma=False,
    )
```

```python
import functools
import math

import jax
import jax.numpy as jnp
from jax import lax
from jax.experimental import pallas as pl
from jax.experimental.pallas import tpu as pltpu
from jax.sharding import PartitionSpec as P

LANES = 128
SOURCE = {1: 0, 2: 0, 4: 0, 3: 2, 5: 4, 7: 6}


def code(value):
    top = jnp.maximum(jnp.max(jnp.abs(value), axis=0, keepdims=True), 1e-30)
    whole = jnp.round(value * (32767.0 / top))
    return whole.astype(jnp.int32).astype(jnp.int16), top * (1.0 / 32767.0)


def decode(whole, unit):
    return whole.astype(jnp.int32).astype(jnp.float32) * unit


def fused(
    n_cells, ndata, units, order, chunks, aligned,
    slots_in, live_in, jac_in, basis_in, weights_in, residual_in,
    jq_out, system_out, rhs_out,
    slots, live, weights, residual, jq, system, rhs,
    own_basis, peer_basis, gy, jac, xq, xs, xrq, xrs, zrq, zrs, acc, uq, us, ut, right, v,
    tq, tcol, gbufs, sbufs, vr,
    in_s, b_s, b_r, y_s, y_r, w_s, w_r, x_s, x_r, z_s, z_r, u_s, u_r, t_s, t_r,
    vz_s, vz_r, g_sems, s_sems,
):
    f32 = jnp.float32
    half = n_cells // 2
    tile = jac.shape[1]
    slot_count = jac.shape[2] // tile
    width = basis_in.shape[2]
    full = uq.shape[2]
    own_rows = system.shape[0]
    k_half = own_basis.shape[0] // 2
    window = vr.shape[2]
    me, cell = lax.axis_index("dp"), lax.axis_index("cells")
    core, y = me % 2, me // 2
    core_peer = y * 2 + 1 - core
    y_peer = (1 - y) * 2 + core
    far_peer = (1 - y) * 2 + 1 - core
    sources = (me, core_peer, y_peer, far_peer)
    x, line = cell % 2, cell // 2
    x_cell = line * 2 + 1 - x

    def remote(src, dst, send, recv, dp, to_cell):
        return pltpu.make_async_remote_copy(
            src_ref=src, dst_ref=dst, send_sem=send, recv_sem=recv,
            device_id=(dp, to_cell), device_id_type=pl.DeviceIdType.MESH,
        )

    def pair(src, dst, send, recv, at, to, dp, to_cell):
        return [
            remote(src[i], dst[i], send.at[(i, *at)], recv.at[(i, *to)], dp, to_cell)
            for i in range(2)
        ]

    def each(verb, copies):
        for copy in copies:
            getattr(copy, verb)()

    def when(condition, run):
        if condition is None:
            run()
        else:
            pl.when(condition)(run)

    load_basis = pltpu.make_async_copy(basis_in, own_basis, in_s.at[0])
    load_jac = pltpu.make_async_copy(jac_in, jac, in_s.at[1])
    load_basis.start()
    small = [
        pltpu.make_async_copy(src, dst, in_s.at[2 + i])
        for i, (src, dst) in enumerate((
            (weights_in, weights), (residual_in, residual), (slots_in, slots), (live_in, live)
        ))
    ]
    each("start", small)
    load_jac.start()

    barrier = pltpu.get_barrier_semaphore()
    for dp in sources:
        for to_cell in (cell, x_cell):
            if dp is me and to_cell is cell:
                continue
            pl.semaphore_signal(
                barrier, inc=1, device_id=(dp, to_cell), device_id_type=pl.DeviceIdType.MESH
            )

    @pl.loop(1, half)
    def _(k):
        pl.semaphore_signal(
            barrier, inc=1, device_id=(me, (line + k) % half * 2 + x),
            device_id_type=pl.DeviceIdType.MESH,
        )

    pl.semaphore_wait(barrier, 7 + half - 1)

    def half_of(ref, side):
        return ref.at[pl.ds(side * k_half, k_half)]

    def y_part(ref, p):
        return ref.at[pl.ds(core * k_half, k_half), :, pl.ds(p * LANES, LANES)]

    def y_copy(src, p, q):
        return remote(
            src, half_of(gy[p][q], core), y_s.at[p, q], y_r.at[p, q], y_peer, cell
        )

    def y_own(verb, p, q):
        pl.when(core == q)(lambda: each(verb, [y_copy(y_part(own_basis, p), p, q)]))

    def y_other(verb, p, q):
        pl.when(core != q)(lambda: each(verb, [y_copy(y_part(peer_basis, p), p, q)]))

    def swap(p, q, side):
        piece = half_of(gy[p][q], side)
        return remote(piece, piece, w_s.at[p, q], w_r.at[p, q], core_peer, cell)

    to_core = remote(own_basis, peer_basis, b_s.at[0], b_r.at[0], core_peer, cell)

    load_basis.wait()
    for q in range(2):
        y_own("start", order[0], q)
    to_core.start()

    square = (tile, tile)

    def column(row):
        return jnp.transpose(jnp.broadcast_to(row, square))

    v[...] = jnp.zeros_like(v)
    each("wait", small)
    root = jnp.sqrt(weights[...])
    tq[0] = root * residual[...]
    wcol = column(root)[:, 0:1]
    tcol[0] = column(tq[0])

    t_targets = [
        (s, sources[(s // 4) * 2 + s % 2], x_cell if s // 2 % 2 else cell) for s in range(1, 8)
    ]
    t_copies = [
        remote(tq.at[0], tq.at[s], t_s.at[s], t_r.at[s], dp, to_cell)
        for s, dp, to_cell in t_targets
    ]
    each("start", t_copies)
    load_jac.wait()

    def lanes(n, dy=0, dc=0, sub=None):
        r, first, size = units[n]
        oy = 1 - y if dy else y
        oc = 1 - core if dc else core
        group = (oy * 2 + oc, oy * 2 + 1 - oc, (1 - oy) * 2, (1 - oy) * 2 + 1)[r]
        if sub is not None:
            first, size = first + sub[0], sub[1]
        return pl.ds(pl.multiple_of(group * width + first, LANES), size)

    def block_dot(n, b):
        r, first, size = units[n]
        held = (own_basis, peer_basis)[r] if r < 2 else gy[first // LANES][r - 2]
        if n == 0:
            for t in range(slot_count):
                at = slice(t * tile, (t + 1) * tile)
                keep = jnp.minimum(jnp.maximum(live[b] - t, 0), 1).astype(f32)
                jac[b, :, at] = jac[b, :, at] * keep.astype(jac.dtype)
        rows = [held[slots[b, t]] for t in range(slot_count)]
        return jnp.dot(jac[b], jnp.concatenate(rows, axis=0), preferred_element_type=f32)

    def part(refs, n, j):
        r, first, size = units[n]
        return [ref.at[r, j, :, first:first + size] for ref in refs]

    def x_copy(n, j):
        return pair(
            part((xq, xs), n, j), part((xrq, xrs), n, j), x_s, x_r, (n, j), (n, j), me, x_cell
        )

    def z_copy(n, j, slot):
        return pair(
            part((xrq, xrs), n, j), part((zrq, zrs), n, slot),
            z_s, z_r, (n, j), (n, slot), me, 2 * j + x,
        )

    def send_x(n):
        r, first, size = units[n]

        @pl.loop(0, half, unroll=1)
        def _(j):
            value, unit = code(block_dot(n, 2 * j + 1 - x))
            xq[r, j, :, first:first + size] = value
            xs[r, j, :, first:first + size] = unit
            each("start", x_copy(n, j))

    def send_z(n):
        r, first, size = units[n]
        cols = slice(first, first + size)

        def total(j):
            value = block_dot(n, 2 * j + x)
            each("wait_recv", x_copy(n, j))
            return value + decode(xrq[r, j, :, cols], xrs[r, j, :, cols])

        @pl.loop(1, half, unroll=1)
        def _(k):
            j = (line + k) % half
            value, unit = code(total(j))
            xrq[r, j, :, cols] = value
            xrs[r, j, :, cols] = unit
            each("start", z_copy(n, j, line))

        acc[r, :, cols] = total(line)

    def pass_on(p, q):
        y_copy(half_of(gy[p][q], core), p, q).wait_recv()
        swap(p, q, core).start()

    count = len(units)
    late = range(6, count)

    def part_held(slot, n, at_x):
        r, first, size = units[n]
        sub, condition = None, None
        if aligned:
            if slot in (2, 3) and r >= 2 and first != LANES:
                condition = first != 2 * LANES * (1 - at_x)
            if slot >= 4 and r < 2:
                sub = (at_x * LANES, 2 * LANES)
        return sub, condition

    def u_do(verb, n, slot):
        source, dp, to_cell = SOURCE.get(slot), core_peer, cell
        if slot == 2:
            dp, to_cell = me, x_cell
        elif slot == 4:
            dp = y_peer
        elif slot == 6 and n < 2:
            source, dp = 2, y_peer
        elif slot == 6 and n not in late:
            source, dp, to_cell = 4, me, x_cell
        elif slot == 6:
            source, dp, to_cell = 0, y_peer, x_cell
        if verb == "wait_recv":
            source = slot
        at_x = 1 - x if to_cell is x_cell and verb != "wait_recv" else x
        sub, condition = part_held(slot, n, at_x)
        cols = lanes(n, source // 4, source % 2, sub)

        def run():
            refs = [[ref.at[k, :, cols] for ref in (uq, us)] for k in (source, slot)]
            each(verb, pair(*refs, u_s, u_r, (slot, n), (slot, n), dp, to_cell))

        when(condition, run)

    place = {p: i * LANES for i, p in enumerate(order)}

    def turn(slot, first, size):
        cols = pl.ds(pl.multiple_of(first, LANES), size)
        value = decode(uq[slot, :, cols], us[slot, :, cols])
        term = value * tcol[slot][:, 0:1]
        v[:, cols] = v[:, cols] + jnp.sum(term.reshape(tile // 8, 8, size), axis=0)
        turned = jnp.transpose(value)
        high = turned.astype(jnp.bfloat16)
        at = slice(slot * tile, (slot + 1) * tile)
        ut[cols, at] = high
        at = slice((8 + slot) * tile, (9 + slot) * tile)
        ut[cols, at] = (turned - high.astype(f32)).astype(jnp.bfloat16)

    def own_columns(slot, p):
        cols = pl.ds(pl.multiple_of(me * width + p * LANES, LANES), LANES)
        value = decode(uq[slot, :, cols], us[slot, :, cols])
        high = value.astype(jnp.bfloat16)
        at = slice(place[p], place[p] + LANES)
        for k in (slot, 8 + slot):
            right[k * tile:(k + 1) * tile, at] = high
        right[(16 + slot) * tile:(17 + slot) * tile, at] = (
            value - high.astype(f32)
        ).astype(jnp.bfloat16)

    def take(n, slot):
        r, first, size = units[n]
        dy, dc = slot // 4, slot % 2
        oy, oc = (1 - y if dy else y), (1 - core if dc else core)
        start = (oy * 2 + oc, oy * 2 + 1 - oc, (1 - oy) * 2, (1 - oy) * 2 + 1)[r] * width + first
        if not aligned:
            turn(slot, start, size)
        elif r < 2:
            turn(slot, start + x * LANES, 2 * LANES)
        elif first == LANES:
            turn(slot, start, size)
        else:
            pl.when(first == 2 * LANES * x)(lambda: turn(slot, start, size))
        if r < 2 and not dy and r == dc:
            for p in order:
                own_columns(slot, p)
        if r >= 2 and dy:
            pl.when(core == r - 2)(lambda: own_columns(slot, first // LANES))

    def finish_rows(n):
        r, first, size = units[n]
        cols = slice(first, first + size)

        @pl.loop(1, half, unroll=3)
        def _(k):
            j = (line + k) % half
            each("wait_recv", z_copy(n, j, j))
            acc[r, :, cols] = acc[r, :, cols] + decode(
                zrq[r, j, :, cols], zrs[r, j, :, cols]
            )

        total = acc[r, :, cols]
        out = lanes(n)
        jq[:, out] = total
        scaled = total * wcol
        value, unit = code(scaled)
        uq[0, :, out] = value
        us[0, :, out] = unit
        for slot in (4, 6, 1) if n in late else (4, 1):
            u_do("start", n, slot)

    def arrived(n):
        swap(units[n][1] // LANES, units[n][0] - 2, 1 - core).wait_recv()

    def out_x(n):
        u_do("start", n, 2)

    def relay_y(n):
        u_do("wait_recv", n, 4)
        if 2 <= n and n not in late:
            u_do("start", n, 6)
        u_do("start", n, 5)

    def relay_x(n):
        u_do("wait_recv", n, 2)
        if n < 2:
            u_do("start", n, 6)
        u_do("start", n, 3)

    def relay_xy(n):
        u_do("wait_recv", n, 6)
        u_do("start", n, 7)

    def take_near(n):
        take(n, 0)
        u_do("wait_recv", n, 1)
        for slot in (1, 2, 4, 6):
            take(n, slot)

    def take_rest(n):
        for slot in (3, 5, 7):
            u_do("wait_recv", n, slot)
            take(n, slot)

    def to_rows(n):
        if n == 1:
            to_core.wait_recv()
            for q in range(2):
                y_other("start", order[0], q)
            for p in order[1:]:
                for q in range(2):
                    y_own("start", p, q)
                    y_other("start", p, q)
        if n >= 2:
            arrived(n)
        send_x(n)

    def on(n):
        p, q = units[n][1] // LANES, units[n][0] - 2
        if p != order[0]:
            pass_on(p, q)
            return
        for k in range(2):
            pl.when(core == k if q == 0 else core != k)(lambda: pass_on(p, k))

    def row_start(j):
        return (2 * j + x) * own_rows

    def window_start(j):
        return jnp.minimum(row_start(j) // LANES * LANES, full - window)

    def g_copy(i, j, slot):
        gq, gs, grq, grs = gbufs[i][1:]
        send, recv = g_sems[i]
        return pair(
            (gq.at[j], gs.at[j]), (grq.at[slot], grs.at[slot]), send, recv, (j,), (slot,),
            me, 2 * j + x,
        )

    def first_row(i, j):
        kind, _, _, rows = chunks[i]
        start = {"outer": j * width + 2 * x * LANES, "inner": j * width + LANES + x * rows,
                 "all": row_start(j)}[kind]
        return pl.ds(pl.multiple_of(start, 16), rows)

    def times_right(i, left):
        _, first, size, _ = chunks[i]
        at, deep = slice(first, first + size), 8 * tile
        value = jnp.dot(left(2 * deep), right[0:2 * deep, at], preferred_element_type=f32)
        return value + jnp.dot(left(deep), right[2 * deep:, at], preferred_element_type=f32)

    def product(i):
        _, _, size, rows = chunks[i]
        value = times_right(i, lambda depth: jnp.concatenate(
            [ut[first_row(i, j), 0:depth] for j in range(half)], axis=0
        ))
        gbufs[i][0][...] = value.reshape(half, rows, size)

    def line_product(i, j):
        gbufs[i][0][j] = times_right(i, lambda depth: ut[first_row(i, j), 0:depth])

    def own_place(i):
        kind, _, _, rows = chunks[i]
        if kind == "all":
            return pl.ds(0, rows)
        at = (x if kind == "outer" else 1 - x) * (own_rows - rows)
        return pl.ds(pl.multiple_of(at, 8), rows)

    def spans(i):
        _, first, size, _ = chunks[i]
        for p in order:
            if first <= place[p] < first + size:
                at = place[p] - first
                yield slice(p * LANES, (p + 1) * LANES), slice(at, at + LANES)

    def gram(i, by_line=False):
        if not by_line:
            product(i)

        @pl.loop(1, half, unroll=1 if by_line else 3)
        def _(k):
            j = (line + k) % half
            if by_line:
                line_product(i, j)
            gq, gs = gbufs[i][1:3]
            value, unit = code(gbufs[i][0][j])
            gq[j] = value
            gs[j] = unit * (1.0 / ndata)
            each("start", g_copy(i, j, line))

    def s_pair(i, k):
        src, dst, dp = ((0, 1, core_peer), (0, 2, y_peer), (2, 3, core_peer))[k]
        sq, su = sbufs[i]
        send, recv = s_sems[i]
        return pair(
            (sq.at[src], su.at[src]), (sq.at[dst], su.at[dst]), send, recv, (k,), (k,), dp, cell
        )

    def s_sum(i):
        total = gbufs[i][0]
        grq, grs = gbufs[i][3:]
        total[line] = total[line] * (1.0 / ndata)

        @pl.loop(1, half, unroll=3)
        def _(k):
            j = (line + k) % half
            each("wait_recv", g_copy(i, j, j))
            total[line] = total[line] + decode(grq[j], grs[j])

        sq, su = sbufs[i]
        sq[0], su[0] = code(total[line])
        each("start", s_pair(i, 1))
        each("start", s_pair(i, 0))

    def s_relay(i):
        each("wait_recv", s_pair(i, 1))
        each("start", s_pair(i, 2))

    def s_finish(i, r):
        rows = chunks[i][3]
        sq, su = sbufs[i]
        at = own_place(i)
        row = lax.broadcasted_iota(jnp.int32, (rows, LANES), 0) + cell * own_rows + at.start
        col = lax.broadcasted_iota(jnp.int32, (rows, LANES), 1) + sources[r] * width
        for to, part in spans(i):
            value = decode(sq[r, :, part], su[r, :, part])
            out = pl.ds(pl.multiple_of(sources[r] * width + to.start, LANES), LANES)
            system[at, out] = value + (row == col + to.start).astype(f32)

    def vz_copy(j, slot):
        at = pl.ds(pl.multiple_of(window_start(j), LANES), window)
        return remote(v.at[:, at], vr.at[slot], vz_s.at[j], vz_r.at[slot], me, 2 * j + x)

    to_rows(0)
    to_rows(1)
    send_z(0)
    on(2)
    on(3)
    to_rows(3)
    send_z(1)
    on(4)
    to_rows(2)
    finish_rows(0)
    to_rows(4)
    send_z(3)
    on(5)
    to_rows(5)
    send_z(4)
    out_x(0)
    finish_rows(3)
    send_z(2)
    on(6)
    to_rows(6)
    send_z(5)
    finish_rows(4)
    finish_rows(1)
    out_x(1)
    finish_rows(2)
    relay_x(0)
    out_x(3)
    on(7)
    out_x(4)
    to_rows(7)
    send_z(6)
    finish_rows(5)
    relay_x(1)
    relay_y(3)
    relay_x(3)
    relay_y(4)
    relay_x(4)
    relay_y(0)
    out_x(2)
    relay_y(2)
    send_z(7)
    out_x(5)
    relay_y(1)
    relay_y(5)
    finish_rows(6)
    relay_xy(3)
    for s in range(1, 8):
        t_copies[s - 1].wait_recv()
        tcol[s] = column(tq[s])
    take_near(3)
    relay_xy(1)
    take_near(1)
    relay_xy(0)
    relay_xy(2)
    relay_xy(4)
    relay_x(2)
    take_near(0)
    take_near(2)
    out_x(6)
    relay_x(5)
    take_rest(1)
    relay_xy(5)
    take_near(4)
    take_near(5)
    finish_rows(7)
    take_rest(0)
    take_rest(3)
    take_rest(4)
    take_rest(2)
    out_x(7)
    take_rest(5)
    if aligned:
        gram(0, by_line=True)
    relay_y(7)
    relay_y(6)
    relay_x(6)
    relay_xy(6)
    relay_x(7)
    relay_xy(7)
    take_near(6)
    take_near(7)
    take_rest(6)
    take_rest(7)
    put_jq = pltpu.make_async_copy(jq, jq_out, in_s.at[6])
    put_jq.start()
    rest = range(1 if aligned else 0, len(chunks))
    for i in rest:
        gram(i, by_line=True)

    @pl.loop(1, half)
    def _(k):
        vz_copy((line + k) % half, line).start()

    if aligned:
        line_product(0, line)
        s_sum(0)
        s_finish(0, 0)
        s_relay(0)

    for i in rest:
        line_product(i, line)
        s_sum(i)

    vr[line] = v[:, pl.ds(pl.multiple_of(window_start(line), LANES), window)]
    total = vr[line]
    for k in range(1, half):
        j = (line + k) % half
        vz_copy(j, j).wait_recv()
        total = total + vr[j]
    misfit = jnp.sum(total, axis=0, keepdims=True) / math.sqrt(ndata)
    offset = row_start(line) - window_start(line)
    own = jnp.zeros(rhs.shape, f32)
    starts = [c * own_rows for c in range(n_cells)]
    for off in sorted({s - min(s // LANES * LANES, full - window) for s in starts}):
        own = jnp.where(offset == off, misfit[:, off:off + own_rows], own)
    rhs[...] = own

    put_rhs = pltpu.make_async_copy(rhs, rhs_out, in_s.at[7])
    put_rhs.start()
    if aligned:
        each("wait_recv", s_pair(0, 0))
        s_finish(0, 1)
        s_finish(0, 2)
        each("wait_recv", s_pair(0, 2))
        s_finish(0, 3)
    for i in rest:
        s_finish(i, 0)
        each("wait_recv", s_pair(i, 0))
        s_finish(i, 1)
    for i in rest:
        s_relay(i)
        s_finish(i, 2)
    for i in rest:
        each("wait_recv", s_pair(i, 2))
        s_finish(i, 3)

    put_system = pltpu.make_async_copy(system, system_out, in_s.at[8])
    put_system.start()
    to_core.wait_send()
    for p in order:
        for q in range(2):
            y_own("wait_send", p, q)
            y_other("wait_send", p, q)
            swap(p, q, core).wait_send()
    for n in range(count):
        for slot in range(1, 8):
            u_do("wait_send", n, slot)
    each("wait_send", t_copies)
    for i in range(len(chunks)):
        for k in range(3):
            each("wait_send", s_pair(i, k))

    @pl.loop(0, half)
    def _(j):
        for n in range(count):
            each("wait_send", x_copy(n, j))

    @pl.loop(1, half)
    def _(k):
        j = (line + k) % half
        for n in range(count):
            each("wait_send", z_copy(n, j, line))
        for i in range(len(chunks)):
            each("wait_send", g_copy(i, j, line))
        vz_copy(j, line).wait_send()

    put_jq.wait()
    put_rhs.wait()
    put_system.wait()


def hand_over(parts, *refs):
    count = len(refs) // 3
    sems = refs[-1]
    steps = []
    for i in range(count):
        source, to, held = refs[i], refs[count + i], refs[2 * count + i]
        rows = source.shape[0] // parts[i]
        for k in range(parts[i]):
            at = pl.ds(k * rows, rows)
            n = len(steps)
            steps.append((
                pltpu.make_async_copy(source.at[at], held.at[at], sems.at[0, n]),
                pltpu.make_async_copy(held.at[at], to.at[at], sems.at[1, n]),
            ))
    for read, _ in steps:
        read.start()
    for read, write in steps:
        read.wait()
        write.start()
    for _, write in steps:
        write.wait()


def on_device(jac_blocks, slot_cell_blocks, live_counts, eigen_basis, weights, residual):
    n_cells = lax.axis_size("cells")
    n_groups = lax.axis_size("dp")
    half = n_cells // 2
    tile = jac_blocks.shape[1]
    depth, width = eigen_basis.shape
    full = width * n_groups
    rows_here = full // n_cells
    ndata = weights.shape[0] * n_cells * n_groups
    pieces = width // LANES
    assert n_groups == 4 and n_cells % 2 == 0 and pieces == 3
    assert jac_blocks.shape[0] == n_cells and weights.shape[0] == tile
    aligned = 2 * rows_here == width
    order = (0, 2, 1)
    units = [(0, 0, width), (1, 0, width)]
    for p in order:
        units += [(2, p * LANES, LANES), (3, p * LANES, LANES)]
    window = 2 * LANES
    if aligned:
        chunks = (
            ("outer", 0, 2 * LANES, LANES),
            ("outer", 2 * LANES, LANES, LANES),
            ("inner", 0, width, rows_here - LANES),
        )
    else:
        chunks = (("all", 0, width, rows_here),)
    f32, bf16, i16 = jnp.float32, jnp.bfloat16, jnp.int16
    anywhere = pl.BlockSpec(memory_space=pl.ANY)

    def sems(*shape):
        return [pltpu.SemaphoreType.DMA(shape)] * 2

    def coded(*lead, rows, columns):
        return [pltpu.VMEM((*lead, rows, columns), i16), pltpu.VMEM((*lead, 1, columns), f32)]

    gbufs = tuple(
        (pltpu.VMEM((half, rows, size), f32), *(coded(half, rows=rows, columns=size) * 2))
        for _, _, size, rows in chunks
    )
    blocks = depth // tile
    jq, system, rhs = pl.pallas_call(
        functools.partial(fused, n_cells, ndata, tuple(units), order, chunks, aligned),
        out_shape=(
            jax.ShapeDtypeStruct((tile, full), f32),
            jax.ShapeDtypeStruct((rows_here, full), f32),
            jax.ShapeDtypeStruct((1, rows_here), f32),
        ),
        in_specs=[anywhere] * 6,
        out_specs=(anywhere,) * 3,
        scratch_shapes=[
            pltpu.SMEM(slot_cell_blocks.shape, jnp.int32),
            pltpu.SMEM((live_counts.shape[0],), jnp.int32),
            pltpu.VMEM((1, tile), f32),
            pltpu.VMEM((1, tile), f32),
            pltpu.VMEM((tile, full), f32),
            pltpu.VMEM((rows_here, full), f32),
            pltpu.VMEM((1, rows_here), f32),
            pltpu.VMEM((blocks, tile, width), bf16),
            pltpu.VMEM((blocks, tile, width), bf16),
            ((pltpu.VMEM((blocks, tile, LANES), bf16),) * 2,) * pieces,
            pltpu.VMEM(jac_blocks.shape, bf16),
            *coded(4, half, rows=tile, columns=width),
            *coded(4, half, rows=tile, columns=width),
            *coded(4, half, rows=tile, columns=width),
            pltpu.VMEM((4, tile, width), f32),
            *coded(8, rows=tile, columns=full),
            pltpu.VMEM((full, 16 * tile), bf16),
            pltpu.VMEM((24 * tile, width), bf16),
            pltpu.VMEM((8, full), f32),
            pltpu.VMEM((8, 1, tile), f32),
            pltpu.VMEM((8, tile, tile), f32),
            gbufs,
            tuple(tuple(coded(4, rows=c[3], columns=c[2])) for c in chunks),
            pltpu.VMEM((half, 8, window), f32),
            pltpu.SemaphoreType.DMA((9,)),
            *sems(1), *sems(pieces, 2), *sems(pieces, 2),
            *sems(2, len(units), half), *sems(2, len(units), half),
            *sems(2, 8, len(units)), *sems(8), *sems(half),
            tuple(tuple(sems(2, half)) for _ in chunks),
            tuple(tuple(sems(2, 3)) for _ in chunks),
        ],
        compiler_params=pltpu.CompilerParams(
            collective_id=0, has_side_effects=True, vmem_limit_bytes=60 * 1024 * 1024
        ),
    )(
        slot_cell_blocks, live_counts[:, 0], jac_blocks,
        eigen_basis.reshape(blocks, tile, width), weights[None], residual[None],
    )
    done = (jq, system, rhs)
    parts = tuple(next(k for k in (4, 2, 1) if k == 1 or a.shape[0] % (8 * k) == 0) for a in done)
    jq, system, rhs = pl.pallas_call(
        functools.partial(hand_over, parts),
        out_shape=tuple(jax.ShapeDtypeStruct(a.shape, a.dtype) for a in done),
        in_specs=[anywhere] * 3,
        out_specs=(anywhere,) * 3,
        scratch_shapes=[
            *(pltpu.VMEM(a.shape, a.dtype) for a in done),
            pltpu.SemaphoreType.DMA((2, sum(parts))),
        ],
    )(*done)
    return jq, system, rhs[0]


def solution(mesh):
    placed = (
        P("dp", None, "cells"),
        P("dp", "cells"),
        P("dp", "cells"),
        P("cells", "dp"),
        P(("dp", "cells")),
        P(("dp", "cells")),
    )
    return jax.shard_map(
        on_device,
        mesh=mesh,
        in_specs=placed,
        out_specs=(P(("dp", "cells"), None), P("cells", None), P("cells")),
        check_vma=False,
    )
```
